256 devices in a mesh: freq: 2 (over y_hi), row: 4 (over y_lo, core), blk: 32 (over x, z).
Axes of the slice: x: 4, y: 4 (y_hi: 2, y_lo: 2; y = y_hi * 2 + y_lo), z: 8, core: 2. Of those that a mesh axis runs over, the one named last changes fastest.
Arguments:
- counts: int32 [65536, 8, 128], P(('freq', 'row', 'blk')), parts along dimension 0, may hold values from 0 to 28, as said below
- subspace: bfloat16 [65536, 32], P(('freq', 'row', 'blk')), parts along dimension 0, may hold values from -6 to 6
Outputs:
- modes: float32 [65536, 32], P(('freq', 'row', 'blk')), parts along dimension 0
The draws below stay inside these ranges and needn't reach their ends.
There are 2 independent parts, one for each index of `freq`. The reference program is written for one: setup_inputs(seed, part) draws one part's arguments, and reference() takes and returns one part's arrays. A program takes and returns all parts, laid end to end along the dimension named above; each array names one. Nothing has to cross between parts.
Inputs may be any that keep to these rules, and one draw needn't show every extreme that they name: Integer spike counts.
All inputs are finite; a program needn't handle non-finite values.
Results may differ from the reference program's by a relative error of at most 0.008.
Values may be sent and summed in bfloat16 or wider, within the bound.
No kernel may reach another device: no remote copies, remote signals or barrier semaphores. Data moves between devices by JAX's collectives and lax.ppermute only.
A program may use at most 64 MiB of HBM per device.

```python
import math
import jax
import jax.numpy as jnp
from jax import lax

SEGS = 8
TAPERS = 8
EPOCH_STEPS = 128
SPECTRAL_SLOT = 9
MODES = 32
NEURONS = 32768


def draw_counts(key, part):
    key_top, key_own, key_rhythm, key_weight = jax.random.split(key, 4)
    ceiling = jax.random.randint(key_top, (NEURONS, 1, 1), 2, 21)
    own_noise = jax.random.randint(key_own, (NEURONS, SEGS, EPOCH_STEPS), 0, ceiling)
    rhythm = jax.random.randint(key_rhythm, (MODES, SEGS, EPOCH_STEPS), 0, 4)
    device_clusters = jnp.arange(NEURONS, dtype=jnp.int32) // (NEURONS // MODES)
    weights = jax.random.randint(key_weight, (NEURONS, 1, 1), 0, 4)
    return (own_noise + weights * rhythm[device_clusters]).astype(jnp.int32)


def block_levels(rng, extent, pieces, smallest, high):
    def one(axis_at, parts):
        draws = jax.random.uniform(jax.random.fold_in(jax.random.fold_in(rng, 6), axis_at), (parts,), jnp.float32, smallest / len(pieces), high / len(pieces))
        return jnp.repeat(jnp.exp(draws), extent[axis_at] // parts).reshape((-1,) + (1,) * (len(extent) - axis_at - 1))

    level = one(*pieces[0])
    for cut in pieces[1:]:
        level = level * one(*cut)
    return level


def centred(key, extent, scale, reach, shards=(), held_as=jnp.bfloat16):
    drawn = jax.random.normal(key, extent, jnp.float32) * scale
    if len(shards) > 0:
        drawn = block_levels(key, extent, shards, -0.22, 0.18) * drawn
    return jnp.clip(drawn, min=-reach, max=reach).astype(held_as)


def setup_inputs(seed: int = 0, part: int = 0) -> dict:
    key_of = jax.random.split(jax.random.key(seed), 3)
    part_splits = jax.random.split(jax.random.fold_in(key_of[2], part), 3)
    return {
        "counts": draw_counts(jax.random.fold_in(jax.random.fold_in(key_of[2], part), 71), part),
        "subspace": centred(part_splits[1], (NEURONS, MODES), 1.0, 6.0, ((0, 128),)),
    }


def spectral_table():
    clock_moments = jnp.arange(EPOCH_STEPS, dtype=jnp.float32)
    window_degrees = jnp.arange(TAPERS, dtype=jnp.float32) + 1.0
    prolate_windows = jnp.sqrt(2.0 / (EPOCH_STEPS + 1.0)) * jnp.sin(jnp.pi * (clock_moments[:, None] + 1.0) * window_degrees[None, :] / (EPOCH_STEPS + 1.0))
    oscillation_radians = 2.0 * jnp.pi * SPECTRAL_SLOT * clock_moments / EPOCH_STEPS
    return jnp.concatenate([prolate_windows * jnp.cos(oscillation_radians)[:, None], -prolate_windows * jnp.sin(oscillation_radians)[:, None]], axis=1)

def make_spectra(counts):
    values = counts.astype(jnp.float32)
    centered = values - lax.optimization_barrier(jnp.mean(values, axis=2, keepdims=True))
    height = counts.shape[0]
    flattened = centered.reshape(height * SEGS, EPOCH_STEPS)
    result = jnp.dot(flattened.astype(jnp.float32), spectral_table().astype(jnp.float32), precision=lax.Precision.HIGHEST, preferred_element_type=jnp.float32)
    return result.reshape(height, SEGS * 2 * TAPERS).astype(jnp.bfloat16)

def twist(spectra):
    height = spectra.shape[0]
    pieces_view = spectra.reshape(height, SEGS, 2, TAPERS)
    return jnp.stack([pieces_view[:, :, 1], -pieces_view[:, :, 0]], axis=2).reshape(height, SEGS * 2 * TAPERS)

def inverse_power(spectra):
    widened = spectra.astype(jnp.float32)
    return 1.0 / (lax.optimization_barrier(jnp.sum(widened * widened, axis=1)) + 1e-05)

def tile_image(stacked, inverse_rows, column_spectra, inverse_cols, column_subspace):
    height = inverse_rows.shape[0]
    products = lax.dot_general(stacked.astype(jnp.float32), column_spectra.astype(jnp.float32), (((1,), (1,)), ((), ())), preferred_element_type=jnp.float32)
    real_part = products[:height]
    imag_part = products[height:]
    squared = (real_part * real_part + imag_part * imag_part) * inverse_rows[:, None] * inverse_cols[None, :]
    degrees = float(SEGS * TAPERS)
    coherence = jnp.maximum((degrees * squared - 1.0) / (degrees - 1.0), 0.0).astype(jnp.bfloat16)
    return jnp.dot(coherence.astype(jnp.float32), column_subspace.astype(jnp.float32), preferred_element_type=jnp.float32)

def reference(counts, subspace):
    spectra = make_spectra(counts)
    inverse_factor = inverse_power(spectra)
    twisted = twist(spectra)
    neuron_total = spectra.shape[0]
    rows_per_block = math.gcd(neuron_total, 1024)
    turns = neuron_total // rows_per_block

    def one_block(position):
        offset = (position * rows_per_block).astype(jnp.int32)
        rows_here = lax.dynamic_slice_in_dim(spectra, offset, rows_per_block, 0)
        twist_here = lax.dynamic_slice_in_dim(twisted, offset, rows_per_block, 0)
        inverse_here = lax.dynamic_slice_in_dim(inverse_factor, offset, rows_per_block, 0)
        stacked = jnp.concatenate([rows_here, twist_here], axis=0)
        return tile_image(stacked, inverse_here, spectra, inverse_factor, subspace)
    projected = lax.map(one_block, jnp.arange(turns, dtype=jnp.int32)).reshape(neuron_total, MODES)
    gram = jnp.dot(projected.T.astype(jnp.float32), projected.astype(jnp.float32), precision=lax.Precision.HIGHEST, preferred_element_type=jnp.float32)
    factor = jnp.linalg.cholesky(gram)
    solved = jax.scipy.linalg.solve_triangular(factor, projected.T, lower=True)
    return solved.T * jnp.sqrt(jnp.float32(neuron_total))
```

```python
import functools

import jax
import jax.numpy as jnp
import numpy as np
from jax import lax
from jax.experimental import pallas as pl
from jax.experimental.pallas import tpu as pltpu
from jax.sharding import Mesh
from jax.sharding import PartitionSpec as P

SEGS = 8
TAPERS = 8
EPOCH_STEPS = 128
SPECTRAL_SLOT = 9
MODES = 32
DEGREES = float(SEGS * TAPERS)
COLS = SEGS * 2 * TAPERS
HALF = COLS // 2


def centred_tables():
    t = np.arange(EPOCH_STEPS, dtype=np.float64)
    k = np.arange(TAPERS, dtype=np.float64) + 1.0
    h = np.sqrt(2.0 / (EPOCH_STEPS + 1.0)) * np.sin(np.pi * (t[:, None] + 1.0) * k[None, :] / (EPOCH_STEPS + 1.0))
    turn = 2.0 * np.pi * SPECTRAL_SLOT * t / EPOCH_STEPS
    re = h * np.cos(turn)[:, None]
    im = -h * np.sin(turn)[:, None]
    re = re - re.mean(axis=0, keepdims=True)
    im = im - im.mean(axis=0, keepdims=True)
    full = np.concatenate([np.tile(re, (1, SEGS)), np.tile(im, (1, SEGS))], axis=1)
    parts = []
    rest = full
    for _ in range(3):
        part = rest.astype(jnp.bfloat16)
        parts.append(part)
        rest = rest - part.astype(np.float64)
    return np.stack(parts, axis=0)


def dot(a, b, ca, cb, precision=None):
    return lax.dot_general(
        a, b, (((ca,), (cb,)), ((), ())), precision=precision, preferred_element_type=jnp.float32
    )


def spectra_kernel(counts, subspace, tables, u_ref, w_ref):
    rows = counts.shape[0]
    segment = lax.broadcasted_iota(jnp.int32, (EPOCH_STEPS, COLS), 1) % HALF // TAPERS
    total = jnp.zeros((rows, COLS), jnp.float32)
    for s in range(SEGS):
        x = counts[:, s, :].astype(jnp.float32).astype(jnp.bfloat16)
        for p in range(3):
            t = tables[p]
            t = jnp.where(segment == s, t.astype(jnp.float32), 0.0).astype(jnp.bfloat16)
            total = total + dot(x, t, 1, 0)
    spectra = total.astype(jnp.bfloat16).astype(jnp.float32)
    power = jnp.sum(spectra * spectra, axis=1, keepdims=True) + 1e-05
    scale = jnp.sqrt(np.float32(np.sqrt(DEGREES / (DEGREES - 1.0))) / power)
    u = (spectra * scale).astype(jnp.bfloat16)
    u_ref[...] = u
    w_ref[0:rows, :] = u
    st = subspace[...].astype(jnp.float32).T.astype(jnp.bfloat16)
    for j in range(rows // 128):
        w_ref[rows + MODES * j : rows + MODES * (j + 1), :] = st[:, 128 * j : 128 * (j + 1)]


def twist(u):
    turned = pltpu.roll(u.astype(jnp.float32), HALF, 1)
    lane = lax.broadcasted_iota(jnp.int32, turned.shape, 1)
    return jnp.where(lane < HALF, turned, -turned).astype(jnp.bfloat16)


def image_kernel(shard, step, pieces, has_start, *refs):
    rows_ref = refs[0]
    panels = refs[1 : 1 + pieces]
    start = refs[1 + pieces] if has_start else None
    out = refs[-1]
    packed = shard + shard // 128 * MODES
    total = rows_ref.shape[0]
    for i in range(total // step):
        u = rows_ref[i * step : (i + 1) * step, :]
        t = twist(u)
        acc = start[:, i * step : (i + 1) * step] if has_start else jnp.zeros((MODES, step), jnp.float32)
        for panel in panels:
            for k in range(panel.shape[0] // packed):
                base = k * packed
                w = panel[base : base + shard, :]
                re = dot(u, w, 1, 1)
                im = dot(t, w, 1, 1)
                c = jnp.maximum(re * re + im * im - np.float32(1.0 / (DEGREES - 1.0)), 0.0).astype(jnp.bfloat16)
                st = jnp.concatenate(
                    [
                        panel[base + shard + MODES * j : base + shard + MODES * (j + 1), :]
                        for j in range(shard // 128)
                    ],
                    axis=1,
                )
                acc = acc + dot(st, c, 1, 1)
        out[:, i * step : (i + 1) * step] = acc


def image(rows, panels, shard, start=None, name="image"):
    n = rows.shape[0]
    operands = (rows, *panels) + (() if start is None else (start,))
    cols = sum(p.shape[0] for p in panels) * 4 // 5
    return pl.pallas_call(
        functools.partial(image_kernel, shard, min(1024, n), len(panels), start is not None),
        out_shape=jax.ShapeDtypeStruct((MODES, n), jnp.float32),
        name=name,
        cost_estimate=pl.CostEstimate(
            flops=2 * n * cols * (2 * COLS + 4 * MODES), bytes_accessed=n * 256 + cols * 320, transcendentals=0
        ),
    )(*operands)


def split_kernel(count, *refs):
    a, b = refs[0], refs[1]
    width = a.shape[1] // count
    for k in range(count):
        refs[2 + k][...] = a[:, k * width : (k + 1) * width] + b[:, k * width : (k + 1) * width]


def add_and_split(a, b, count):
    width = a.shape[1] // count
    return pl.pallas_call(
        functools.partial(split_kernel, count),
        out_shape=[jax.ShapeDtypeStruct((a.shape[0], width), jnp.float32)] * count,
        name="add_and_split",
    )(a, b)


def pack(g):
    return jnp.concatenate([g[8 * q : 8 * q + 8, :] for q in range(4)], axis=1)


def unpack(g):
    return jnp.concatenate([g[:, 32 * q : 32 * q + 32] for q in range(4)], axis=0)


def gram_kernel(count, copies, *refs):
    total = refs[0][...]
    for k in range(1, count):
        total = total + refs[k][...]
    refs[count][...] = total
    g = pack(dot(total, total, 1, 1, lax.Precision.HIGHEST))
    for k in range(copies):
        refs[count + 1][k] = g


def gram_of(parts, copies):
    return pl.pallas_call(
        functools.partial(gram_kernel, len(parts), copies),
        out_shape=[
            jax.ShapeDtypeStruct(parts[0].shape, jnp.float32),
            jax.ShapeDtypeStruct((copies, 8, 128), jnp.float32),
        ],
        name="gram",
    )(*parts)


def sum_kernel(copies, g, out):
    total = jnp.sum(g[...], axis=0)
    for k in range(copies):
        out[k] = total


def sum_copies(g, copies):
    return pl.pallas_call(
        functools.partial(sum_kernel, copies),
        out_shape=jax.ShapeDtypeStruct((copies, 8, 128), jnp.float32),
        name="gram_sum",
    )(g)


def modes_kernel(scale, grams, image_ref, out):
    g = unpack(jnp.sum(grams[...], axis=0))
    n = image_ref.shape[1]
    y = image_ref[...]
    row = lax.broadcasted_iota(jnp.int32, (MODES, 1), 0)
    for k in range(MODES):
        inv = 1.0 / jnp.sqrt(g[k : k + 1, k : k + 1])
        pivot_g = g[k : k + 1, :] * inv
        pivot_y = y[k : k + 1, :] * inv
        below = jnp.where(row > k, g[:, k : k + 1] * inv, 0.0)
        g = g - below * pivot_g
        y = jnp.where(row == k, pivot_y, y - below * pivot_y)
    out[...] = (y * scale).T


def modes_of(grams, img, scale):
    return pl.pallas_call(
        functools.partial(modes_kernel, scale),
        out_shape=jax.ShapeDtypeStruct((img.shape[1], MODES), jnp.float32),
        name="modes",
    )(grams, img)


def local(sizes, counts, subspace):
    ny, nc, nx, nz = sizes
    shard = counts.shape[0]
    neurons = shard * ny * nc * nx * nz
    u, w = pl.pallas_call(
        spectra_kernel,
        out_shape=[
            jax.ShapeDtypeStruct((shard, COLS), jnp.bfloat16),
            jax.ShapeDtypeStruct((shard + shard // 128 * MODES, COLS), jnp.bfloat16),
        ],
        name="spectra",
    )(counts, subspace, jnp.asarray(centred_tables()))

    def from_x(v, k):
        return lax.ppermute(v, "x", [((i + k) % nx, i) for i in range(nx)])

    def to_x(v, k):
        return lax.ppermute(v, "x", [(i, (i + k) % nx) for i in range(nx)])

    def swap(v, axis):
        return lax.ppermute(v, axis, [(0, 1), (1, 0)])

    def both_ways(v):
        pairs = [(z, (z + 1) % nz) for z in range(nz)] + [(nz + z, nz + (z - 1) % nz) for z in range(nz)]
        return lax.ppermute(v, ("c", "z"), pairs)

    rows_own = jnp.concatenate([u] + [from_x(u, k) for k in range(1, nx)], axis=0)
    pair = jnp.concatenate([w, swap(w, "c")], axis=0)
    rows_other = swap(rows_own, "y")
    panels = [pair]
    hop = pair
    for k in range(1, nz // 2):
        hop = both_ways(hop)
        panels += [hop, swap(hop, "c")]
    panels.append(both_ways(hop))

    other = image(rows_other, panels, shard, name="image_other")
    mine = image(rows_own, panels, shard, name="image_own")
    sums = add_and_split(mine, swap(other, "y"), nx)
    parts = [sums[0]] + [to_x(sums[k], k) for k in range(1, nx)]
    img, grams = gram_of(parts, ny * nc * nx)
    grams = lax.all_to_all(grams, ("y", "c", "x"), 0, 0)
    grams = sum_copies(grams, nz)
    grams = lax.all_to_all(grams, "z", 0, 0)
    return modes_of(grams, img, float(np.sqrt(neurons)))


def solution(mesh):
    fine = Mesh(mesh.devices.reshape(2, 2, 2, 4, 8), ("freq", "y", "c", "x", "z"))
    every = ("freq", "y", "c", "x", "z")
    return jax.shard_map(
        functools.partial(local, (2, 2, 4, 8)),
        mesh=fine,
        in_specs=(P(every, None, None), P(every, None)),
        out_specs=P(every, None),
        check_vma=False,
    )
```

```python
import functools

import jax
import jax.numpy as jnp
import numpy as np
from jax import lax
from jax.experimental import pallas as pl
from jax.experimental.pallas import tpu as pltpu
from jax.sharding import Mesh
from jax.sharding import PartitionSpec as P

SEGS = 8
TAPERS = 8
EPOCH_STEPS = 128
SPECTRAL_SLOT = 9
MODES = 32
DEGREES = float(SEGS * TAPERS)
COLS = SEGS * 2 * TAPERS
HALF = COLS // 2

SMALL = pltpu.CompilerParams(vmem_limit_bytes=8 << 20)
LARGE = pltpu.CompilerParams(vmem_limit_bytes=24 << 20)


def centred_tables():
    t = np.arange(EPOCH_STEPS, dtype=np.float64)
    k = np.arange(TAPERS, dtype=np.float64) + 1.0
    h = np.sqrt(2.0 / (EPOCH_STEPS + 1.0)) * np.sin(np.pi * (t[:, None] + 1.0) * k[None, :] / (EPOCH_STEPS + 1.0))
    turn = 2.0 * np.pi * SPECTRAL_SLOT * t / EPOCH_STEPS
    re = h * np.cos(turn)[:, None]
    im = -h * np.sin(turn)[:, None]
    re = re - re.mean(axis=0, keepdims=True)
    im = im - im.mean(axis=0, keepdims=True)
    full = np.concatenate([np.tile(re, (1, SEGS)), np.tile(im, (1, SEGS))], axis=1)
    parts = []
    rest = full
    for _ in range(3):
        part = rest.astype(jnp.bfloat16)
        parts.append(part)
        rest = rest - part.astype(np.float64)
    return np.stack(parts, axis=0)


def dot(a, b, ca, cb, precision=None):
    return lax.dot_general(
        a, b, (((ca,), (cb,)), ((), ())), precision=precision, preferred_element_type=jnp.float32
    )


def spectra_kernel(counts, subspace, tables, u_ref, w_ref):
    rows = counts.shape[0]
    segment = lax.broadcasted_iota(jnp.int32, (EPOCH_STEPS, COLS), 1) % HALF // TAPERS
    total = jnp.zeros((rows, COLS), jnp.float32)
    for s in range(SEGS):
        x = counts[:, s, :].astype(jnp.float32).astype(jnp.bfloat16)
        for p in range(3):
            t = tables[p]
            t = jnp.where(segment == s, t.astype(jnp.float32), 0.0).astype(jnp.bfloat16)
            total = total + dot(x, t, 1, 0)
    spectra = total.astype(jnp.bfloat16).astype(jnp.float32)
    power = jnp.sum(spectra * spectra, axis=1, keepdims=True) + 1e-05
    scale = jnp.sqrt(np.float32(np.sqrt(DEGREES / (DEGREES - 1.0))) / power)
    u = (spectra * scale).astype(jnp.bfloat16)
    u_ref[...] = u
    w_ref[0:rows, :] = u
    st = subspace[...]
    for j in range(rows // 128):
        w_ref[rows + MODES * j : rows + MODES * (j + 1), :] = st[:, 128 * j : 128 * (j + 1)]


def twist(u):
    turned = pltpu.roll(u.astype(jnp.float32), HALF, 1)
    lane = lax.broadcasted_iota(jnp.int32, turned.shape, 1)
    return jnp.where(lane < HALF, turned, -turned).astype(jnp.bfloat16)


def image_kernel(shard, step, pieces, has_start, *refs):
    rows_ref = refs[0]
    panels = refs[1 : 1 + pieces]
    start = refs[1 + pieces] if has_start else None
    out = refs[-1]
    packed = shard + shard // 128 * MODES
    total = rows_ref.shape[0]
    for i in range(total // step):
        u = rows_ref[i * step : (i + 1) * step, :]
        t = twist(u)
        acc = start[:, i * step : (i + 1) * step] if has_start else jnp.zeros((MODES, step), jnp.float32)
        for panel in panels:
            for k in range(panel.shape[0] // packed):
                base = k * packed
                w = panel[base : base + shard, :]
                re = dot(u, w, 1, 1)
                im = dot(t, w, 1, 1)
                c = jnp.maximum(re * re + im * im - np.float32(1.0 / (DEGREES - 1.0)), 0.0).astype(jnp.bfloat16)
                st = jnp.concatenate(
                    [
                        panel[base + shard + MODES * j : base + shard + MODES * (j + 1), :]
                        for j in range(shard // 128)
                    ],
                    axis=1,
                )
                acc = acc + dot(st, c, 1, 1)
        out[:, i * step : (i + 1) * step] = acc


def image(rows, panels, shard, start=None, name="image"):
    n = rows.shape[0]
    operands = (rows, *panels) + (() if start is None else (start,))
    cols = sum(p.shape[0] for p in panels) * 4 // 5
    return pl.pallas_call(
        functools.partial(image_kernel, shard, min(1024, n), len(panels), start is not None),
        out_shape=jax.ShapeDtypeStruct((MODES, n), jnp.float32),
        compiler_params=LARGE,
        name=name,
        cost_estimate=pl.CostEstimate(
            flops=2 * n * cols * (2 * COLS + 4 * MODES), bytes_accessed=n * 256 + cols * 320, transcendentals=0
        ),
    )(*operands)


def split_kernel(count, *refs):
    a, b = refs[0], refs[1]
    width = a.shape[1] // count
    for k in range(count):
        refs[2 + k][...] = a[:, k * width : (k + 1) * width] + b[:, k * width : (k + 1) * width]


def add_and_split(a, b, count):
    width = a.shape[1] // count
    return pl.pallas_call(
        functools.partial(split_kernel, count),
        out_shape=[jax.ShapeDtypeStruct((a.shape[0], width), jnp.float32)] * count,
        compiler_params=SMALL,
        name="add_and_split",
    )(a, b)


def pack(g):
    return jnp.concatenate([g[8 * q : 8 * q + 8, :] for q in range(4)], axis=1)


def unpack(g):
    return jnp.concatenate([g[:, 32 * q : 32 * q + 32] for q in range(4)], axis=0)


def gram_kernel(count, *refs):
    total = refs[0][...]
    for k in range(1, count):
        total = total + refs[k][...]
    refs[count][...] = total
    refs[count + 1][...] = pack(dot(total, total, 1, 1, lax.Precision.HIGHEST))


def gram_of(parts):
    return pl.pallas_call(
        functools.partial(gram_kernel, len(parts)),
        out_shape=[
            jax.ShapeDtypeStruct(parts[0].shape, jnp.float32),
            jax.ShapeDtypeStruct((8, 128), jnp.float32),
        ],
        compiler_params=SMALL,
        name="gram",
    )(*parts)


def sum_kernel(count, copies, *refs):
    total = (refs[0][...] + refs[1][...]) + (refs[2][...] + refs[3][...])
    for k in range(copies):
        refs[count][k] = total


def sum_copies(grams, copies):
    return pl.pallas_call(
        functools.partial(sum_kernel, len(grams), copies),
        out_shape=jax.ShapeDtypeStruct((copies, 8, 128), jnp.float32),
        compiler_params=SMALL,
        name="gram_sum",
    )(*grams)


def modes_kernel(scale, grams, image_ref, out):
    g = unpack(jnp.sum(grams[...], axis=0))
    n = image_ref.shape[1]
    y = image_ref[...]
    row = lax.broadcasted_iota(jnp.int32, (MODES, 1), 0)
    for k in range(MODES):
        pivot = g[k : k + 1, k : k + 1]
        inv = lax.rsqrt(pivot)
        inv = inv * (1.5 - 0.5 * pivot * inv * inv)
        pivot_g = g[k : k + 1, :] * inv
        pivot_y = y[k : k + 1, :] * inv
        below = jnp.where(row > k, g[:, k : k + 1] * inv, 0.0)
        g = g - below * pivot_g
        y = jnp.where(row == k, pivot_y, y - below * pivot_y)
    out[...] = y * scale


def modes_of(grams, img, scale):
    return pl.pallas_call(
        functools.partial(modes_kernel, scale),
        out_shape=jax.ShapeDtypeStruct((MODES, img.shape[1]), jnp.float32),
        compiler_params=SMALL,
        name="modes",
    )(grams, img)


def local(sizes, counts, subspace):
    ny, nc, nx, nz = sizes
    shard = counts.shape[0]
    neurons = shard * ny * nc * nx * nz
    u, w = pl.pallas_call(
        spectra_kernel,
        out_shape=[
            jax.ShapeDtypeStruct((shard, COLS), jnp.bfloat16),
            jax.ShapeDtypeStruct((shard + shard // 128 * MODES, COLS), jnp.bfloat16),
        ],
        compiler_params=LARGE,
        name="spectra",
    )(counts, subspace.T, jnp.asarray(centred_tables()))

    def from_x(v, k):
        return lax.ppermute(v, "x", [((i + k) % nx, i) for i in range(nx)])

    def to_x(v, k):
        return lax.ppermute(v, "x", [(i, (i + k) % nx) for i in range(nx)])

    def swap(v, axis):
        return lax.ppermute(v, axis, [(0, 1), (1, 0)])

    def both_ways(v, k):
        pairs = [(z, (z + k) % nz) for z in range(nz)] + [(nz + z, nz + (z - k) % nz) for z in range(nz)]
        return lax.ppermute(v, ("c", "z"), pairs)

    pair = jnp.concatenate([w, swap(w, "c")], axis=0)
    one = both_ways(pair, 1)
    two = both_ways(pair, 2)
    rows_own = jnp.concatenate([u] + [from_x(u, k) for k in range(1, nx)], axis=0)
    rows_other = swap(rows_own, "y")
    early = [pair, one, swap(one, "c"), two, swap(two, "c")]
    three = both_ways(two, 1)
    late = [three, swap(three, "c"), both_ways(two, 2)]

    mine = image(rows_own, early, shard, name="own_early")
    mine, rows_other = lax.optimization_barrier((mine, rows_other))
    other = image(rows_other, early, shard, name="other_early")
    other, *late = lax.optimization_barrier((other, *late))
    other = image(rows_other, late, shard, start=other, name="other_late")
    mine = image(rows_own, late, shard, start=mine, name="own_late")
    sums = add_and_split(mine, swap(other, "y"), nx)
    parts = [sums[0]] + [to_x(sums[k], k) for k in range(1, nx)]
    img, gram = gram_of(parts)
    quad = ("y", "c")
    four = [gram] + [lax.ppermute(gram, quad, [(i, i ^ k) for i in range(4)]) for k in (1, 2, 3)]
    grams = sum_copies(four, nx * nz)
    grams = lax.all_to_all(grams, ("x", "z"), 0, 0)
    return modes_of(grams, img, float(np.sqrt(neurons))).T


def solution(mesh):
    fine = Mesh(mesh.devices.reshape(2, 2, 2, 4, 8), ("freq", "y", "c", "x", "z"))
    every = ("freq", "y", "c", "x", "z")
    return jax.shard_map(
        functools.partial(local, (2, 2, 4, 8)),
        mesh=fine,
        in_specs=(P(every, None, None), P(every, None)),
        out_specs=P(every, None),
        check_vma=False,
    )
```

```python
import functools

import jax
import jax.numpy as jnp
import numpy as np
from jax import lax
from jax.experimental import pallas as pl
from jax.experimental.pallas import tpu as pltpu
from jax.sharding import Mesh
from jax.sharding import PartitionSpec as P

SEGS = 8
TAPERS = 8
EPOCH_STEPS = 128
SPECTRAL_SLOT = 9
MODES = 32
DEGREES = float(SEGS * TAPERS)
COLS = SEGS * 2 * TAPERS
HALF = COLS // 2

SMALL = pltpu.CompilerParams(vmem_limit_bytes=8 << 20)
WHOLE = pltpu.CompilerParams(vmem_limit_bytes=60 * 1024 * 1024)
LARGE = pltpu.CompilerParams(vmem_limit_bytes=24 << 20)


def centred_tables():
    t = np.arange(EPOCH_STEPS, dtype=np.float64)
    k = np.arange(TAPERS, dtype=np.float64) + 1.0
    h = np.sqrt(2.0 / (EPOCH_STEPS + 1.0)) * np.sin(np.pi * (t[:, None] + 1.0) * k[None, :] / (EPOCH_STEPS + 1.0))
    turn = 2.0 * np.pi * SPECTRAL_SLOT * t / EPOCH_STEPS
    re = h * np.cos(turn)[:, None]
    im = -h * np.sin(turn)[:, None]
    re = re - re.mean(axis=0, keepdims=True)
    im = im - im.mean(axis=0, keepdims=True)
    full = np.concatenate([np.tile(re, (1, SEGS)), np.tile(im, (1, SEGS))], axis=1)
    parts = []
    rest = full
    for _ in range(3):
        part = rest.astype(jnp.bfloat16)
        parts.append(part)
        rest = rest - part.astype(np.float64)
    return np.stack(parts, axis=0)


def dot(a, b, ca, cb, precision=None):
    return lax.dot_general(
        a, b, (((ca,), (cb,)), ((), ())), precision=precision, preferred_element_type=jnp.float32
    )


CHUNKS = 4


def spectra_kernel(counts_hbm, subspace_hbm, tables_hbm, u_ref, w_ref, counts, subspace, tables, sems):
    rows = counts.shape[0]
    part = rows // CHUNKS
    copies = [pltpu.make_async_copy(tables_hbm, tables, sems.at[CHUNKS])]
    for i in range(CHUNKS):
        span = pl.ds(i * part, part)
        copies.append(pltpu.make_async_copy(counts_hbm.at[span], counts.at[span], sems.at[i]))
    copies.append(pltpu.make_async_copy(subspace_hbm, subspace, sems.at[CHUNKS + 1]))
    for copy in copies:
        copy.start()
    segment = lax.broadcasted_iota(jnp.int32, (EPOCH_STEPS, COLS), 1) % HALF // TAPERS
    copies[0].wait()
    table = [
        [jnp.where(segment == s, tables[p].astype(jnp.float32), 0.0).astype(jnp.bfloat16) for p in range(3)]
        for s in range(SEGS)
    ]
    for i in range(CHUNKS):
        copies[1 + i].wait()
        span = slice(i * part, (i + 1) * part)
        total = jnp.zeros((part, COLS), jnp.float32)
        for s in range(SEGS):
            x = counts[span, s, :].astype(jnp.float32).astype(jnp.bfloat16)
            for p in range(3):
                total = total + dot(x, table[s][p], 1, 0)
        spectra = total.astype(jnp.bfloat16).astype(jnp.float32)
        power = jnp.sum(spectra * spectra, axis=1, keepdims=True) + 1e-05
        scale = jnp.sqrt(np.float32(np.sqrt(DEGREES / (DEGREES - 1.0))) / power)
        u = (spectra * scale).astype(jnp.bfloat16)
        u_ref[span, :] = u
        w_ref[span, :] = u
    copies[-1].wait()
    for j in range(rows // 128):
        w_ref[rows + MODES * j : rows + MODES * (j + 1), :] = subspace[:, 128 * j : 128 * (j + 1)]


def twist(u):
    turned = pltpu.roll(u.astype(jnp.float32), HALF, 1)
    lane = lax.broadcasted_iota(jnp.int32, turned.shape, 1)
    return jnp.where(lane < HALF, turned, -turned).astype(jnp.bfloat16)


def image_kernel(shard, step, pieces, has_start, *refs):
    rows_ref = refs[0]
    panels = refs[1 : 1 + pieces]
    start = refs[1 + pieces] if has_start else None
    out = refs[-1]
    packed = shard + shard // 128 * MODES
    total = rows_ref.shape[0]
    for i in range(total // step):
        u = rows_ref[i * step : (i + 1) * step, :]
        t = twist(u)
        acc = start[:, i * step : (i + 1) * step] if has_start else jnp.zeros((MODES, step), jnp.float32)
        for panel in panels:
            for k in range(panel.shape[0] // packed):
                base = k * packed
                w = panel[base : base + shard, :]
                re = dot(u, w, 1, 1)
                im = dot(t, w, 1, 1)
                c = jnp.maximum(re * re + im * im - np.float32(1.0 / (DEGREES - 1.0)), 0.0).astype(jnp.bfloat16)
                st = jnp.concatenate(
                    [
                        panel[base + shard + MODES * j : base + shard + MODES * (j + 1), :]
                        for j in range(shard // 128)
                    ],
                    axis=1,
                )
                acc = acc + dot(st, c, 1, 1)
        out[:, i * step : (i + 1) * step] = acc


def image(rows, panels, shard, start=None):
    n = rows.shape[0]
    operands = (rows, *panels) + (() if start is None else (start,))
    cols = sum(p.shape[0] for p in panels) * 4 // 5
    return image_call(n, operands, cols, panels, shard, start)


def image_call(n, operands, cols, panels, shard, start):
    return pl.pallas_call(
        functools.partial(image_kernel, shard, min(1024, n), len(panels), start is not None),
        out_shape=jax.ShapeDtypeStruct((MODES, n), jnp.float32),
        compiler_params=LARGE,
        cost_estimate=pl.CostEstimate(
            flops=2 * n * cols * (2 * COLS + 4 * MODES), bytes_accessed=n * 256 + cols * 320, transcendentals=0
        ),
    )(*operands)


def split_kernel(count, *refs):
    a, b = refs[0], refs[1]
    width = a.shape[1] // count
    for k in range(count):
        refs[2 + k][...] = a[:, k * width : (k + 1) * width] + b[:, k * width : (k + 1) * width]


def add_and_split(a, b, count):
    width = a.shape[1] // count
    return pl.pallas_call(
        functools.partial(split_kernel, count),
        out_shape=[jax.ShapeDtypeStruct((a.shape[0], width), jnp.float32)] * count,
        compiler_params=SMALL,
        name="add_and_split",
    )(a, b)


def pack(g):
    return jnp.concatenate([g[8 * q : 8 * q + 8, :] for q in range(4)], axis=1)


def unpack(g):
    return jnp.concatenate([g[:, 32 * q : 32 * q + 32] for q in range(4)], axis=0)


def gram_kernel(count, *refs):
    total = refs[0][...]
    for k in range(1, count):
        total = total + refs[k][...]
    refs[count][...] = total
    refs[count + 1][...] = pack(dot(total, total, 1, 1, lax.Precision.HIGHEST))


def gram_of(parts):
    return pl.pallas_call(
        functools.partial(gram_kernel, len(parts)),
        out_shape=[
            jax.ShapeDtypeStruct(parts[0].shape, jnp.float32),
            jax.ShapeDtypeStruct((8, 128), jnp.float32),
        ],
        compiler_params=SMALL,
        name="gram",
    )(*parts)


def sum_kernel(count, copies, *refs):
    total = (refs[0][...] + refs[1][...]) + (refs[2][...] + refs[3][...])
    for k in range(copies):
        refs[count][k] = total


def sum_copies(grams, copies):
    return pl.pallas_call(
        functools.partial(sum_kernel, len(grams), copies),
        out_shape=jax.ShapeDtypeStruct((copies, 8, 128), jnp.float32),
        compiler_params=SMALL,
        name="gram_sum",
    )(*grams)


def modes_kernel(scale, grams, image_ref, out):
    g = unpack(jnp.sum(grams[...], axis=0))
    y = image_ref[...]
    row = lax.broadcasted_iota(jnp.int32, (MODES, 1), 0)
    for k in range(MODES):
        pivot = g[k : k + 1, k : k + 1]
        inv = lax.rsqrt(pivot)
        inv = inv * (1.5 - 0.5 * pivot * inv * inv)
        pivot_g = g[k : k + 1, :] * inv
        pivot_y = y[k : k + 1, :] * inv
        below = jnp.where(row > k, g[:, k : k + 1] * inv, 0.0)
        g = g - below * pivot_g
        y = jnp.where(row == k, pivot_y, y - below * pivot_y)
    out[...] = y * scale


def modes_of(grams, img, scale):
    return pl.pallas_call(
        functools.partial(modes_kernel, scale),
        out_shape=jax.ShapeDtypeStruct((MODES, img.shape[1]), jnp.float32),
        compiler_params=SMALL,
        name="modes",
    )(grams, img)


def local(sizes, counts, subspace):
    ny, nc, nx, nz = sizes
    shard = counts.shape[0]
    neurons = shard * ny * nc * nx * nz
    u, w = pl.pallas_call(
        spectra_kernel,
        out_shape=[
            jax.ShapeDtypeStruct((shard, COLS), jnp.bfloat16),
            jax.ShapeDtypeStruct((shard + shard // 128 * MODES, COLS), jnp.bfloat16),
        ],
        in_specs=[pl.BlockSpec(memory_space=pltpu.HBM)] * 3,
        scratch_shapes=[
            pltpu.VMEM(counts.shape, jnp.int32),
            pltpu.VMEM((MODES, shard), jnp.bfloat16),
            pltpu.VMEM((3, EPOCH_STEPS, COLS), jnp.bfloat16),
            pltpu.SemaphoreType.DMA((CHUNKS + 2,)),
        ],
        compiler_params=WHOLE,
        name="spectra",
    )(counts, subspace.T, jnp.asarray(centred_tables()))

    def from_x(v, k):
        return lax.ppermute(v, "x", [((i + k) % nx, i) for i in range(nx)])

    def to_x(v, k):
        return lax.ppermute(v, "x", [(i, (i + k) % nx) for i in range(nx)])

    def swap(v, axis):
        return lax.ppermute(v, axis, [(0, 1), (1, 0)])

    def both_ways(v, k):
        pairs = [(z, (z + k) % nz) for z in range(nz)] + [(nz + z, nz + (z - k) % nz) for z in range(nz)]
        return lax.ppermute(v, ("c", "z"), pairs)

    pair = jnp.concatenate([w, swap(w, "c")], axis=0)
    rows_own = jnp.concatenate([u] + [from_x(u, k) for k in range(1, nx)], axis=0)
    rows_other = swap(rows_own, "y")
    one = both_ways(pair, 1)
    three = both_ways(pair, 3)
    one_c = swap(one, "c")
    two = both_ways(one, 1)
    three_c = swap(three, "c")
    four = both_ways(three, 1)
    two_c = swap(two, "c")
    mine = image(rows_own, [pair], shard)
    mine = image(rows_own, [one, one_c], shard, start=mine)
    other = image(rows_other, [pair, one, one_c, three, three_c], shard)
    other = image(rows_other, [two, two_c, four], shard, start=other)
    mine = image(rows_own, [three, three_c, two, two_c, four], shard, start=mine)
    sums = add_and_split(mine, swap(other, "y"), nx)
    parts = [sums[0]] + [to_x(sums[k], k) for k in range(1, nx)]
    img, gram = gram_of(parts)
    quad = ("y", "c")
    four = [gram] + [lax.ppermute(gram, quad, [(i, i ^ k) for i in range(4)]) for k in (1, 2, 3)]
    grams = sum_copies(four, nx * nz)
    grams = lax.all_to_all(grams, ("x", "z"), 0, 0)
    return modes_of(grams, img, float(np.sqrt(neurons))).T


def solution(mesh):
    fine = Mesh(mesh.devices.reshape(2, 2, 2, 4, 8), ("freq", "y", "c", "x", "z"))
    every = ("freq", "y", "c", "x", "z")

    def body(counts, subspace):
        return local((2, 2, 4, 8), counts, subspace)

    return jax.shard_map(
        body,
        mesh=fine,
        in_specs=(P(every, None, None), P(every, None)),
        out_specs=P(every, None),
        check_vma=False,
    )
```

```python
import functools

import jax
import jax.numpy as jnp
import numpy as np
from jax import lax
from jax.experimental import pallas as pl
from jax.experimental.pallas import tpu as pltpu
from jax.sharding import Mesh
from jax.sharding import PartitionSpec as P

SEGS = 8
TAPERS = 8
EPOCH_STEPS = 128
SPECTRAL_SLOT = 9
MODES = 32
DEGREES = float(SEGS * TAPERS)
COLS = SEGS * 2 * TAPERS
HALF = COLS // 2

SMALL = pltpu.CompilerParams(vmem_limit_bytes=8 << 20)
LARGE = pltpu.CompilerParams(vmem_limit_bytes=24 << 20)


def centred_tables():
    t = np.arange(EPOCH_STEPS, dtype=np.float64)
    k = np.arange(TAPERS, dtype=np.float64) + 1.0
    h = np.sqrt(2.0 / (EPOCH_STEPS + 1.0)) * np.sin(np.pi * (t[:, None] + 1.0) * k[None, :] / (EPOCH_STEPS + 1.0))
    turn = 2.0 * np.pi * SPECTRAL_SLOT * t / EPOCH_STEPS
    re = h * np.cos(turn)[:, None]
    im = -h * np.sin(turn)[:, None]
    re = re - re.mean(axis=0, keepdims=True)
    im = im - im.mean(axis=0, keepdims=True)
    full = np.concatenate([np.tile(re, (1, SEGS)), np.tile(im, (1, SEGS))], axis=1)
    parts = []
    rest = full
    for _ in range(3):
        part = rest.astype(jnp.bfloat16)
        parts.append(part)
        rest = rest - part.astype(np.float64)
    return np.stack(parts, axis=0)


def dot(a, b, ca, cb, precision=None):
    return lax.dot_general(
        a, b, (((ca,), (cb,)), ((), ())), precision=precision, preferred_element_type=jnp.float32
    )


CHUNKS = 4


def spectra_kernel(counts_hbm, subspace_hbm, tables_hbm, u_ref, w_ref, counts, subspace, tables, sems):
    rows = counts.shape[0]
    part = rows // CHUNKS
    copies = [pltpu.make_async_copy(tables_hbm, tables, sems.at[CHUNKS])]
    for i in range(CHUNKS):
        span = pl.ds(i * part, part)
        copies.append(pltpu.make_async_copy(counts_hbm.at[span], counts.at[span], sems.at[i]))
    copies.append(pltpu.make_async_copy(subspace_hbm, subspace, sems.at[CHUNKS + 1]))
    for copy in copies:
        copy.start()
    segment = lax.broadcasted_iota(jnp.int32, (EPOCH_STEPS, COLS), 1) % HALF // TAPERS
    copies[0].wait()
    table = [
        [jnp.where(segment == s, tables[p].astype(jnp.float32), 0.0).astype(jnp.bfloat16) for p in range(3)]
        for s in range(SEGS)
    ]
    for i in range(CHUNKS):
        copies[1 + i].wait()
        span = slice(i * part, (i + 1) * part)
        total = jnp.zeros((part, COLS), jnp.float32)
        for s in range(SEGS):
            x = counts[span, s, :].astype(jnp.float32).astype(jnp.bfloat16)
            for p in range(3):
                total = total + dot(x, table[s][p], 1, 0)
        spectra = total.astype(jnp.bfloat16).astype(jnp.float32)
        power = jnp.sum(spectra * spectra, axis=1, keepdims=True) + 1e-05
        scale = jnp.sqrt(np.float32(np.sqrt(DEGREES / (DEGREES - 1.0))) / power)
        u = (spectra * scale).astype(jnp.bfloat16)
        u_ref[span, :] = u
        w_ref[span, :] = u
    copies[-1].wait()
    for j in range(rows // 128):
        w_ref[rows + MODES * j : rows + MODES * (j + 1), :] = subspace[:, 128 * j : 128 * (j + 1)]


def twist(u):
    turned = pltpu.roll(u.astype(jnp.float32), HALF, 1)
    lane = lax.broadcasted_iota(jnp.int32, turned.shape, 1)
    return jnp.where(lane < HALF, turned, -turned).astype(jnp.bfloat16)


def image_kernel(shard, halves, blocks, pieces, has_start, *refs):
    rows = refs[:blocks]
    panels = refs[blocks : blocks + pieces]
    starts = refs[blocks + pieces : blocks + pieces + len(halves)] if has_start else ()
    outs = refs[-len(halves) :]
    packed = shard + shard // 128 * MODES
    for h, half in enumerate(halves):
        u = jnp.concatenate([r[half * shard : (half + 1) * shard, :] for r in rows], axis=0)
        t = twist(u)
        acc = starts[h][...] if has_start else jnp.zeros((MODES, blocks * shard), jnp.float32)
        for panel in panels:
            for k in range(panel.shape[0] // packed):
                base = k * packed
                w = panel[base : base + shard, :]
                re = dot(u, w, 1, 1)
                im = dot(t, w, 1, 1)
                c = jnp.maximum(re * re + im * im - np.float32(1.0 / (DEGREES - 1.0)), 0.0).astype(jnp.bfloat16)
                st = jnp.concatenate(
                    [
                        panel[base + shard + MODES * j : base + shard + MODES * (j + 1), :]
                        for j in range(shard // 128)
                    ],
                    axis=1,
                )
                acc = acc + dot(st, c, 1, 1)
        outs[h][...] = acc


def image(rows, halves, panels, shard, starts=()):
    n = len(rows) * shard
    cols = sum(p.shape[0] for p in panels) * 4 // 5
    return pl.pallas_call(
        functools.partial(image_kernel, shard, halves, len(rows), len(panels), len(starts) > 0),
        out_shape=[jax.ShapeDtypeStruct((MODES, n), jnp.float32)] * len(halves),
        compiler_params=LARGE,
        cost_estimate=pl.CostEstimate(
            flops=2 * n * len(halves) * cols * (2 * COLS + 4 * MODES),
            bytes_accessed=n * 256 + cols * 320,
            transcendentals=0,
        ),
    )(*rows, *panels, *starts)


def split_kernel(count, *refs):
    a, b = refs[0], refs[1]
    width = a.shape[1] // count
    for k in range(count):
        refs[2 + k][...] = a[:, k * width : (k + 1) * width] + b[:, k * width : (k + 1) * width]


def add_and_split(a, b, count):
    width = a.shape[1] // count
    return pl.pallas_call(
        functools.partial(split_kernel, count),
        out_shape=[jax.ShapeDtypeStruct((a.shape[0], width), jnp.float32)] * count,
        compiler_params=SMALL,
        name="add_and_split",
    )(a, b)


def pack(g):
    return jnp.concatenate([g[8 * q : 8 * q + 8, :] for q in range(4)], axis=1)


def unpack(g):
    return jnp.concatenate([g[:, 32 * q : 32 * q + 32] for q in range(4)], axis=0)


def gram_kernel(count, *refs):
    total = refs[0][...]
    for k in range(1, count):
        total = total + refs[k][...]
    refs[count][...] = total
    refs[count + 1][...] = pack(dot(total, total, 1, 1, lax.Precision.HIGHEST))


def gram_of(parts):
    return pl.pallas_call(
        functools.partial(gram_kernel, len(parts)),
        out_shape=[
            jax.ShapeDtypeStruct(parts[0].shape, jnp.float32),
            jax.ShapeDtypeStruct((8, 128), jnp.float32),
        ],
        compiler_params=SMALL,
        name="gram",
    )(*parts)


def sum_kernel(count, copies, *refs):
    total = (refs[0][...] + refs[1][...]) + (refs[2][...] + refs[3][...])
    for k in range(copies):
        refs[count][k] = total


def sum_copies(grams, copies):
    return pl.pallas_call(
        functools.partial(sum_kernel, len(grams), copies),
        out_shape=jax.ShapeDtypeStruct((copies, 8, 128), jnp.float32),
        compiler_params=SMALL,
        name="gram_sum",
    )(*grams)


def modes_kernel(scale, grams, image_ref, out):
    g = unpack(jnp.sum(grams[...], axis=0))
    y = image_ref[...]
    row = lax.broadcasted_iota(jnp.int32, (MODES, 1), 0)
    for k in range(MODES):
        pivot = g[k : k + 1, k : k + 1]
        inv = lax.rsqrt(pivot)
        inv = inv * (1.5 - 0.5 * pivot * inv * inv)
        pivot_g = g[k : k + 1, :] * inv
        pivot_y = y[k : k + 1, :] * inv
        below = jnp.where(row > k, g[:, k : k + 1] * inv, 0.0)
        g = g - below * pivot_g
        y = jnp.where(row == k, pivot_y, y - below * pivot_y)
    out[...] = y * scale


def modes_of(grams, img, scale):
    return pl.pallas_call(
        functools.partial(modes_kernel, scale),
        out_shape=jax.ShapeDtypeStruct((MODES, img.shape[1]), jnp.float32),
        compiler_params=SMALL,
        name="modes",
    )(grams, img)


def local(sizes, counts, subspace):
    ny, nc, nx, nz = sizes
    shard = counts.shape[0]
    neurons = shard * ny * nc * nx * nz
    u, w = pl.pallas_call(
        spectra_kernel,
        out_shape=[
            jax.ShapeDtypeStruct((shard, COLS), jnp.bfloat16),
            jax.ShapeDtypeStruct((shard + shard // 128 * MODES, COLS), jnp.bfloat16),
        ],
        in_specs=[pl.BlockSpec(memory_space=pltpu.HBM)] * 3,
        scratch_shapes=[
            pltpu.VMEM(counts.shape, jnp.int32),
            pltpu.VMEM((MODES, shard), jnp.bfloat16),
            pltpu.VMEM((3, EPOCH_STEPS, COLS), jnp.bfloat16),
            pltpu.SemaphoreType.DMA((CHUNKS + 2,)),
        ],
        compiler_params=LARGE,
        name="spectra",
    )(*(pltpu.with_memory_space_constraint(v, pltpu.HBM) for v in (counts, subspace.T, jnp.asarray(centred_tables()))))

    def from_x(v, k):
        return lax.ppermute(v, "x", [((i + k) % nx, i) for i in range(nx)])

    def to_x(v, k):
        return lax.ppermute(v, "x", [(i, (i + k) % nx) for i in range(nx)])

    def swap(v, axis):
        return lax.ppermute(v, axis, [(0, 1), (1, 0)])

    def both_ways(v, k):
        pairs = [(z, (z + k) % nz) for z in range(nz)] + [(nz + z, nz + (z - k) % nz) for z in range(nz)]
        return lax.ppermute(v, ("c", "z"), pairs)

    first = jnp.concatenate([u, swap(u, "y")], axis=0)
    pair = jnp.concatenate([w, swap(w, "c")], axis=0)
    one = both_ways(pair, 1)
    two = both_ways(pair, 2)
    rows = [first] + [from_x(first, k) for k in range(1, nx)]
    one_c = swap(one, "c")
    two_c = swap(two, "c")
    far = both_ways(jnp.concatenate([one, two], axis=0), 2)
    far_c = swap(far[: pair.shape[0]], "c")
    own, other = image(rows, (0, 1), [pair, one, one_c], shard)
    (other,) = image(rows, (1,), [two, two_c], shard, (other,))
    (own,) = image(rows, (0,), [two, two_c], shard, (own,))
    (other,) = image(rows, (1,), [far, far_c], shard, (other,))
    (own,) = image(rows, (0,), [far, far_c], shard, (own,))
    sums = add_and_split(own, swap(other, "y"), nx)
    parts = [sums[0]] + [to_x(sums[k], k) for k in range(1, nx)]
    img, gram = gram_of(parts)
    quad = ("y", "c")
    four = [gram] + [lax.ppermute(gram, quad, [(i, i ^ k) for i in range(4)]) for k in (1, 2, 3)]
    grams = sum_copies(four, nx * nz)
    grams = lax.all_to_all(grams, ("x", "z"), 0, 0)
    return modes_of(grams, img, float(np.sqrt(neurons))).T


def solution(mesh):
    fine = Mesh(mesh.devices.reshape(2, 2, 2, 4, 8), ("freq", "y", "c", "x", "z"))
    every = ("freq", "y", "c", "x", "z")

    def body(counts, subspace):
        return local((2, 2, 4, 8), counts, subspace)

    return jax.shard_map(
        body,
        mesh=fine,
        in_specs=(P(every, None, None), P(every, None)),
        out_specs=P(every, None),
        check_vma=False,
    )
```

```python
import functools

import jax
import jax.numpy as jnp
import numpy as np
from jax import lax
from jax.experimental import pallas as pl
from jax.experimental.pallas import tpu as pltpu
from jax.sharding import Mesh
from jax.sharding import PartitionSpec as P

SEGS = 8
TAPERS = 8
EPOCH_STEPS = 128
SPECTRAL_SLOT = 9
MODES = 32
DEGREES = float(SEGS * TAPERS)
COLS = SEGS * 2 * TAPERS
HALF = COLS // 2

SMALL = pltpu.CompilerParams(vmem_limit_bytes=8 << 20)
LARGE = pltpu.CompilerParams(vmem_limit_bytes=24 << 20)


def centred_tables():
    t = np.arange(EPOCH_STEPS, dtype=np.float64)
    k = np.arange(TAPERS, dtype=np.float64) + 1.0
    h = np.sqrt(2.0 / (EPOCH_STEPS + 1.0)) * np.sin(np.pi * (t[:, None] + 1.0) * k[None, :] / (EPOCH_STEPS + 1.0))
    turn = 2.0 * np.pi * SPECTRAL_SLOT * t / EPOCH_STEPS
    re = h * np.cos(turn)[:, None]
    im = -h * np.sin(turn)[:, None]
    re = re - re.mean(axis=0, keepdims=True)
    im = im - im.mean(axis=0, keepdims=True)
    full = np.concatenate([np.tile(re, (1, SEGS)), np.tile(im, (1, SEGS))], axis=1)
    parts = []
    rest = full
    for _ in range(3):
        part = rest.astype(jnp.bfloat16)
        parts.append(part)
        rest = rest - part.astype(np.float64)
    return np.stack(parts, axis=0)


def dot(a, b, ca, cb, precision=None):
    return lax.dot_general(
        a, b, (((ca,), (cb,)), ((), ())), precision=precision, preferred_element_type=jnp.float32
    )


CHUNKS = 4


def spectra_kernel(counts_hbm, subspace_hbm, tables_hbm, u_ref, w_ref, counts, subspace, tables, sems):
    rows = counts.shape[0]
    part = rows // CHUNKS
    copies = [pltpu.make_async_copy(tables_hbm, tables, sems.at[CHUNKS])]
    for i in range(CHUNKS):
        span = pl.ds(i * part, part)
        copies.append(pltpu.make_async_copy(counts_hbm.at[span], counts.at[span], sems.at[i]))
    copies.append(pltpu.make_async_copy(subspace_hbm, subspace, sems.at[CHUNKS + 1]))
    for copy in copies:
        copy.start()
    segment = lax.broadcasted_iota(jnp.int32, (EPOCH_STEPS, COLS), 1) % HALF // TAPERS
    copies[0].wait()
    table = [
        [jnp.where(segment == s, tables[p].astype(jnp.float32), 0.0).astype(jnp.bfloat16) for p in range(3)]
        for s in range(SEGS)
    ]
    for i in range(CHUNKS):
        copies[1 + i].wait()
        span = slice(i * part, (i + 1) * part)
        total = jnp.zeros((part, COLS), jnp.float32)
        for s in range(SEGS):
            x = counts[span, s, :].astype(jnp.float32).astype(jnp.bfloat16)
            for p in range(3):
                total = total + dot(x, table[s][p], 1, 0)
        spectra = total.astype(jnp.bfloat16).astype(jnp.float32)
        power = jnp.sum(spectra * spectra, axis=1, keepdims=True) + 1e-05
        scale = jnp.sqrt(np.float32(np.sqrt(DEGREES / (DEGREES - 1.0))) / power)
        u = (spectra * scale).astype(jnp.bfloat16)
        u_ref[span, :] = u
        w_ref[span, :] = u
    copies[-1].wait()
    for j in range(rows // 128):
        w_ref[rows + MODES * j : rows + MODES * (j + 1), :] = subspace[:, 128 * j : 128 * (j + 1)]


def twist(u):
    turned = pltpu.roll(u.astype(jnp.float32), HALF, 1)
    lane = lax.broadcasted_iota(jnp.int32, turned.shape, 1)
    return jnp.where(lane < HALF, turned, -turned).astype(jnp.bfloat16)


def image_kernel(shard, blocks, pieces, has_start, *refs):
    rows = refs[:blocks]
    panels = refs[blocks : blocks + pieces]
    starts = refs[blocks + pieces : 2 * blocks + pieces] if has_start else ()
    outs = refs[-blocks:]
    packed = shard + shard // 128 * MODES
    u = jnp.concatenate([r[...] for r in rows], axis=0)
    t = twist(u)
    if has_start:
        acc = jnp.concatenate([r[...] for r in starts], axis=1)
    else:
        acc = jnp.zeros((MODES, u.shape[0]), jnp.float32)
    for panel in panels:
        for k in range(panel.shape[0] // packed):
            base = k * packed
            w = panel[base : base + shard, :]
            re = dot(u, w, 1, 1)
            im = dot(t, w, 1, 1)
            c = jnp.maximum(re * re + im * im - np.float32(1.0 / (DEGREES - 1.0)), 0.0).astype(jnp.bfloat16)
            st = jnp.concatenate(
                [panel[base + shard + MODES * j : base + shard + MODES * (j + 1), :] for j in range(shard // 128)],
                axis=1,
            )
            acc = acc + dot(st, c, 1, 1)
    width = rows[0].shape[0]
    for i in range(blocks):
        outs[i][...] = acc[:, i * width : (i + 1) * width]


def image(rows, panels, shard, starts=()):
    n = sum(r.shape[0] for r in rows)
    cols = sum(p.shape[0] for p in panels) * 4 // 5
    return pl.pallas_call(
        functools.partial(image_kernel, shard, len(rows), len(panels), len(starts) > 0),
        out_shape=[jax.ShapeDtypeStruct((MODES, r.shape[0]), jnp.float32) for r in rows],
        compiler_params=LARGE,
        cost_estimate=pl.CostEstimate(
            flops=2 * n * cols * (2 * COLS + 4 * MODES), bytes_accessed=n * 256 + cols * 320, transcendentals=0
        ),
    )(*rows, *panels, *starts)


def add_kernel(*refs):
    total = refs[0][...]
    for r in refs[1:-1]:
        total = total + r[...]
    refs[-1][...] = total


def add(parts):
    return pl.pallas_call(
        add_kernel,
        out_shape=jax.ShapeDtypeStruct(parts[0].shape, jnp.float32),
        compiler_params=SMALL,
        name="add",
    )(*parts)


def pack(g):
    return jnp.concatenate([g[8 * q : 8 * q + 8, :] for q in range(4)], axis=1)


def unpack(g):
    return jnp.concatenate([g[:, 32 * q : 32 * q + 32] for q in range(4)], axis=0)


def gram_kernel(mine, theirs, image_ref, gram_ref):
    half = mine.shape[1] // 2
    own = mine[:, :half] + theirs[:, half:]
    other = mine[:, half:] + theirs[:, :half]
    image_ref[...] = own
    g = dot(own, own, 1, 1, lax.Precision.HIGHEST) + dot(other, other, 1, 1, lax.Precision.HIGHEST)
    gram_ref[...] = pack(g)


def gram_of(mine, theirs):
    return pl.pallas_call(
        gram_kernel,
        out_shape=[
            jax.ShapeDtypeStruct((MODES, mine.shape[1] // 2), jnp.float32),
            jax.ShapeDtypeStruct((8, 128), jnp.float32),
        ],
        compiler_params=SMALL,
        name="gram",
    )(mine, theirs)


def copies_kernel(copies, a, b, out):
    total = a[...] + b[...]
    for k in range(copies):
        out[k] = total


def add_and_copy(a, b, copies):
    return pl.pallas_call(
        functools.partial(copies_kernel, copies),
        out_shape=jax.ShapeDtypeStruct((copies, 8, 128), jnp.float32),
        compiler_params=SMALL,
        name="gram_copies",
    )(a, b)


BLOCK = 4


def modes_kernel(scale, grams, image_ref, out):
    g = unpack(jnp.sum(grams[...], axis=0))
    g = jnp.concatenate([g, jnp.zeros((MODES, 128 - MODES), jnp.float32)], axis=1)
    y = image_ref[...]
    n = y.shape[1]
    for k in range(0, MODES, BLOCK):
        block = [
            [jnp.broadcast_to(g[k + i : k + i + 1, k + j : k + j + 1], (8, 128)) for j in range(i + 1)]
            for i in range(BLOCK)
        ]
        gr = [jnp.broadcast_to(g[k + i : k + i + 1, :], (8, 128)) for i in range(BLOCK)]
        yr = [jnp.broadcast_to(y[k + i : k + i + 1, :], (8, n)) for i in range(BLOCK)]
        gc = [jnp.broadcast_to(g[:, k + i : k + i + 1], (MODES, 128)) for i in range(BLOCK)]
        wide = lambda v: jnp.concatenate([v] * (n // 128), axis=1)
        tall = lambda v: jnp.concatenate([v] * (MODES // 8), axis=0)
        for i in range(BLOCK):
            for j in range(i):
                low = block[i][j]
                for r in range(i, BLOCK):
                    if r == i:
                        block[i][i] = block[i][i] - low * low
                    else:
                        block[r][i] = block[r][i] - block[r][j] * low
                gr[i] = gr[i] - low * gr[j]
                yr[i] = yr[i] - wide(low) * yr[j]
                gc[i] = gc[i] - tall(low) * gc[j]
            pivot = block[i][i]
            inv = lax.rsqrt(pivot)
            inv = inv * (1.5 - 0.5 * pivot * inv * inv)
            for r in range(i + 1, BLOCK):
                block[r][i] = block[r][i] * inv
            gr[i] = gr[i] * inv
            yr[i] = yr[i] * wide(inv)
            gc[i] = gc[i] * tall(inv)
        if k + BLOCK < MODES:
            for i in range(BLOCK):
                g = g - gc[i] * tall(gr[i])
                y = y - wide(gc[i]) * tall(yr[i])
        for i in range(BLOCK):
            out[k + i : k + i + 1, :] = yr[i][0:1, :] * scale


def modes_of(grams, img, scale):
    return pl.pallas_call(
        functools.partial(modes_kernel, scale),
        out_shape=jax.ShapeDtypeStruct((MODES, img.shape[1]), jnp.float32),
        compiler_params=SMALL,
        name="modes",
    )(grams, img)


def local(sizes, counts, subspace):
    ny, nc, nx, nz = sizes
    shard = counts.shape[0]
    neurons = shard * ny * nc * nx * nz
    u, w = pl.pallas_call(
        spectra_kernel,
        out_shape=[
            jax.ShapeDtypeStruct((shard, COLS), jnp.bfloat16),
            jax.ShapeDtypeStruct((shard + shard // 128 * MODES, COLS), jnp.bfloat16),
        ],
        in_specs=[pl.BlockSpec(memory_space=pltpu.HBM)] * 3,
        scratch_shapes=[
            pltpu.VMEM(counts.shape, jnp.int32),
            pltpu.VMEM((MODES, shard), jnp.bfloat16),
            pltpu.VMEM((3, EPOCH_STEPS, COLS), jnp.bfloat16),
            pltpu.SemaphoreType.DMA((CHUNKS + 2,)),
        ],
        compiler_params=LARGE,
        name="spectra",
    )(*(pltpu.with_memory_space_constraint(v, pltpu.HBM) for v in (counts, subspace.T, jnp.asarray(centred_tables()))))

    def from_x(v, k):
        return lax.ppermute(v, "x", [((i + k) % nx, i) for i in range(nx)])

    def to_x(v, k):
        return lax.ppermute(v, "x", [(i, (i + k) % nx) for i in range(nx)])

    def swap(v, axis):
        return lax.ppermute(v, axis, [(0, 1), (1, 0)])

    def both_ways(v, k):
        pairs = [(z, (z + k) % nz) for z in range(nz)] + [(nz + z, nz + (z - k) % nz) for z in range(nz)]
        return lax.ppermute(v, ("c", "z"), pairs)

    first = jnp.concatenate([u, swap(u, "y")], axis=0)
    pair = jnp.concatenate([w, swap(w, "c")], axis=0)
    one = both_ways(pair, 1)
    two = both_ways(pair, 2)
    rows = [first] + [from_x(first, k) for k in range(1, nx)]
    one_c = swap(one, "c")
    two_c = swap(two, "c")
    far = both_ways(jnp.concatenate([one, two[: w.shape[0]]], axis=0), 2)
    far_c = swap(far, "c")
    home, rest = rows[:1], rows[1:]
    near = image(home, [pair], shard)
    near = image(home, [one, one_c, two, two_c], shard, near)
    away = image(rest, [pair, one, one_c], shard)
    away = image(rest, [two, two_c], shard, away)
    away = image(rest, [far], shard, away)
    away = image(rest, [far_c], shard, away)
    back = [to_x(away[k - 1], k) for k in (2, 1, 3)]
    near = image(home, [far, far_c], shard, near)
    mine = add([*near, *back])
    img, gram = gram_of(mine, swap(mine, "y"))
    grams = add_and_copy(gram, swap(gram, "c"), nx * nz)
    grams = lax.all_to_all(grams, ("x", "z"), 0, 0)
    return modes_of(grams, img, float(np.sqrt(neurons))).T


def solution(mesh):
    fine = Mesh(mesh.devices.reshape(2, 2, 2, 4, 8), ("freq", "y", "c", "x", "z"))
    every = ("freq", "y", "c", "x", "z")

    def body(counts, subspace):
        return local((2, 2, 4, 8), counts, subspace)

    return jax.shard_map(
        body,
        mesh=fine,
        in_specs=(P(every, None, None), P(every, None)),
        out_specs=P(every, None),
        check_vma=False,
    )
```

```python
import functools

import jax
import jax.numpy as jnp
import numpy as np
from jax import lax
from jax.experimental import pallas as pl
from jax.experimental.pallas import tpu as pltpu
from jax.sharding import Mesh
from jax.sharding import PartitionSpec as P

SEGS = 8
TAPERS = 8
EPOCH_STEPS = 128
SPECTRAL_SLOT = 9
MODES = 32
DEGREES = float(SEGS * TAPERS)
COLS = SEGS * 2 * TAPERS
HALF = COLS // 2

SMALL = pltpu.CompilerParams(vmem_limit_bytes=8 << 20)
LARGE = pltpu.CompilerParams(vmem_limit_bytes=24 << 20)


def centred_tables():
    t = np.arange(EPOCH_STEPS, dtype=np.float64)
    k = np.arange(TAPERS, dtype=np.float64) + 1.0
    h = np.sqrt(2.0 / (EPOCH_STEPS + 1.0)) * np.sin(np.pi * (t[:, None] + 1.0) * k[None, :] / (EPOCH_STEPS + 1.0))
    turn = 2.0 * np.pi * SPECTRAL_SLOT * t / EPOCH_STEPS
    re = h * np.cos(turn)[:, None]
    im = -h * np.sin(turn)[:, None]
    re = re - re.mean(axis=0, keepdims=True)
    im = im - im.mean(axis=0, keepdims=True)
    full = np.concatenate([np.tile(re, (1, SEGS)), np.tile(im, (1, SEGS))], axis=1)
    parts = []
    rest = full
    for _ in range(3):
        part = rest.astype(jnp.bfloat16)
        parts.append(part)
        rest = rest - part.astype(np.float64)
    return np.stack(parts, axis=0)


def dot(a, b, ca, cb, precision=None):
    return lax.dot_general(
        a, b, (((ca,), (cb,)), ((), ())), precision=precision, preferred_element_type=jnp.float32
    )


CHUNKS = 2


def spectra_kernel(counts_hbm, subspace_hbm, tables_hbm, u_ref, w_ref, counts, subspace, tables, sems):
    rows = counts.shape[0]
    part = rows // CHUNKS
    copies = [pltpu.make_async_copy(tables_hbm, tables, sems.at[CHUNKS])]
    for i in range(CHUNKS):
        span = pl.ds(i * part, part)
        copies.append(pltpu.make_async_copy(counts_hbm.at[span], counts.at[span], sems.at[i]))
    copies.append(pltpu.make_async_copy(subspace_hbm, subspace, sems.at[CHUNKS + 1]))
    for copy in copies:
        copy.start()
    segment = lax.broadcasted_iota(jnp.int32, (EPOCH_STEPS, COLS), 1) % HALF // TAPERS
    copies[0].wait()
    table = [
        [jnp.where(segment == s, tables[p].astype(jnp.float32), 0.0).astype(jnp.bfloat16) for p in range(3)]
        for s in range(SEGS)
    ]
    for i in range(CHUNKS):
        copies[1 + i].wait()
        span = slice(i * part, (i + 1) * part)
        upper = jnp.zeros((part, 2 * COLS), jnp.float32)
        lower = jnp.zeros((part, COLS), jnp.float32)
        for s in range(0, SEGS, 2):
            x = [counts[span, s + j, :].astype(jnp.float32).astype(jnp.bfloat16) for j in range(2)]
            x = jnp.concatenate(x, axis=1)
            t = [jnp.concatenate([table[s][p], table[s + 1][p]], axis=0) for p in range(3)]
            upper = upper + dot(x, jnp.concatenate(t[:2], axis=1), 1, 0)
            lower = lower + dot(x, t[2], 1, 0)
        total = upper[:, :COLS] + (upper[:, COLS:] + lower)
        spectra = total.astype(jnp.bfloat16).astype(jnp.float32)
        power = jnp.sum(spectra * spectra, axis=1, keepdims=True) + 1e-05
        scale = jnp.sqrt(np.float32(np.sqrt(DEGREES / (DEGREES - 1.0))) / power)
        u = (spectra * scale).astype(jnp.bfloat16)
        u_ref[span, :] = u
        w_ref[span, :] = u
    copies[-1].wait()
    for j in range(rows // 128):
        w_ref[rows + MODES * j : rows + MODES * (j + 1), :] = subspace[:, 128 * j : 128 * (j + 1)]


def twist(u):
    turned = pltpu.roll(u.astype(jnp.float32), HALF, 1)
    lane = lax.broadcasted_iota(jnp.int32, turned.shape, 1)
    return jnp.where(lane < HALF, turned, -turned).astype(jnp.bfloat16)


def unpack_panels(panels, shard):
    packed = shard + shard // 128 * MODES
    w, st = [], []
    for panel in panels:
        for base in range(0, panel.shape[0], packed):
            w.append(panel[base : base + shard, :])
            st += [panel[base + shard + MODES * j : base + shard + MODES * (j + 1), :] for j in range(shard // 128)]
    return w, st


def coherence(re, im):
    return jnp.maximum(re * re + im * im - np.float32(1.0 / (DEGREES - 1.0)), 0.0).astype(jnp.bfloat16)


def image_kernel(shard, blocks, pieces, has_start, *refs):
    rows = refs[:blocks]
    panels = refs[blocks : blocks + pieces]
    starts = refs[blocks + pieces : 2 * blocks + pieces] if has_start else ()
    outs = refs[-blocks:]
    u = jnp.concatenate([r[...] for r in rows], axis=0)
    t = twist(u)
    if has_start:
        acc = jnp.concatenate([r[...] for r in starts], axis=1)
    else:
        acc = jnp.zeros((MODES, u.shape[0]), jnp.float32)
    w, st = unpack_panels(panels, shard)
    per = len(st) // len(w)
    if u.shape[0] < 1024:
        w = jnp.concatenate(w, axis=0)
        c = coherence(dot(w, u, 1, 1), dot(w, t, 1, 1))
        acc = acc + dot(jnp.concatenate(st, axis=1), c, 1, 0)
    else:
        for k in range(len(w)):
            c = coherence(dot(u, w[k], 1, 1), dot(t, w[k], 1, 1))
            acc = acc + dot(jnp.concatenate(st[k * per : (k + 1) * per], axis=1), c, 1, 1)
    width = rows[0].shape[0]
    for i in range(blocks):
        outs[i][...] = acc[:, i * width : (i + 1) * width]


def image(rows, panels, shard, starts=()):
    n = sum(r.shape[0] for r in rows)
    cols = sum(p.shape[0] for p in panels) * 4 // 5
    return pl.pallas_call(
        functools.partial(image_kernel, shard, len(rows), len(panels), len(starts) > 0),
        out_shape=[jax.ShapeDtypeStruct((MODES, r.shape[0]), jnp.float32) for r in rows],
        compiler_params=LARGE,
        cost_estimate=pl.CostEstimate(
            flops=2 * n * cols * (2 * COLS + 4 * MODES), bytes_accessed=n * 256 + cols * 320, transcendentals=0
        ),
    )(*rows, *panels, *starts)


def add_kernel(*refs):
    total = refs[0][...]
    for r in refs[1:-1]:
        total = total + r[...]
    refs[-1][...] = total


def add(parts):
    return pl.pallas_call(
        add_kernel,
        out_shape=jax.ShapeDtypeStruct(parts[0].shape, jnp.float32),
        compiler_params=SMALL,
        name="add",
    )(*parts)


def pack(g):
    return jnp.concatenate([g[8 * q : 8 * q + 8, :] for q in range(4)], axis=1)


def unpack(g):
    return jnp.concatenate([g[:, 32 * q : 32 * q + 32] for q in range(4)], axis=0)


def gram_kernel(copies, mine, by_y, by_core, by_both, image_ref, gram_ref):
    half = mine.shape[1] // 2
    own = mine[:, :half] + by_y[:, half:]
    image_ref[...] = own
    sums = jnp.concatenate(
        [
            own,
            mine[:, half:] + by_y[:, :half],
            by_core[:, :half] + by_both[:, half:],
            by_core[:, half:] + by_both[:, :half],
        ],
        axis=1,
    )
    g = pack(dot(sums, sums, 1, 1, lax.Precision.HIGHEST))
    for k in range(copies):
        gram_ref[k] = g


def gram_of(parts, copies):
    return pl.pallas_call(
        functools.partial(gram_kernel, copies),
        out_shape=[
            jax.ShapeDtypeStruct((MODES, parts[0].shape[1] // 2), jnp.float32),
            jax.ShapeDtypeStruct((copies, 8, 128), jnp.float32),
        ],
        compiler_params=SMALL,
        name="gram",
    )(*parts)


BLOCK = 4


def modes_kernel(scale, grams, image_ref, out):
    g = unpack(jnp.sum(grams[...], axis=0))
    g = jnp.concatenate([g, jnp.zeros((MODES, 128 - MODES), jnp.float32)], axis=1)
    y = image_ref[...]
    n = y.shape[1]
    for k in range(0, MODES, BLOCK):
        block = [
            [jnp.broadcast_to(g[k + i : k + i + 1, k + j : k + j + 1], (8, 128)) for j in range(i + 1)]
            for i in range(BLOCK)
        ]
        gr = [jnp.broadcast_to(g[k + i : k + i + 1, :], (8, 128)) for i in range(BLOCK)]
        yr = [jnp.broadcast_to(y[k + i : k + i + 1, :], (8, n)) for i in range(BLOCK)]
        gc = [jnp.broadcast_to(g[:, k + i : k + i + 1], (MODES, 128)) for i in range(BLOCK)]
        wide = lambda v: jnp.concatenate([v] * (n // 128), axis=1)
        tall = lambda v: jnp.concatenate([v] * (MODES // 8), axis=0)
        for i in range(BLOCK):
            for j in range(i):
                low = block[i][j]
                for r in range(i, BLOCK):
                    if r == i:
                        block[i][i] = block[i][i] - low * low
                    else:
                        block[r][i] = block[r][i] - block[r][j] * low
                gr[i] = gr[i] - low * gr[j]
                yr[i] = yr[i] - wide(low) * yr[j]
                gc[i] = gc[i] - tall(low) * gc[j]
            pivot = block[i][i]
            inv = lax.rsqrt(pivot)
            inv = inv * (1.5 - 0.5 * pivot * inv * inv)
            for r in range(i + 1, BLOCK):
                block[r][i] = block[r][i] * inv
            gr[i] = gr[i] * inv
            yr[i] = yr[i] * wide(inv)
            gc[i] = gc[i] * tall(inv)
        if k + BLOCK < MODES:
            for i in range(BLOCK):
                g = g - gc[i] * tall(gr[i])
                y = y - wide(gc[i]) * tall(yr[i])
        for i in range(BLOCK):
            out[k + i : k + i + 1, :] = yr[i][0:1, :] * scale


def modes_of(grams, img, scale):
    return pl.pallas_call(
        functools.partial(modes_kernel, scale),
        out_shape=jax.ShapeDtypeStruct((MODES, img.shape[1]), jnp.float32),
        compiler_params=SMALL,
        name="modes",
    )(grams, img)


def local(sizes, counts, subspace):
    ny, nc, nx, nz = sizes
    shard = counts.shape[0]
    neurons = shard * ny * nc * nx * nz
    u, w = pl.pallas_call(
        spectra_kernel,
        out_shape=[
            jax.ShapeDtypeStruct((shard, COLS), jnp.bfloat16),
            jax.ShapeDtypeStruct((shard + shard // 128 * MODES, COLS), jnp.bfloat16),
        ],
        in_specs=[pl.BlockSpec(memory_space=pltpu.HBM)] * 3,
        scratch_shapes=[
            pltpu.VMEM(counts.shape, jnp.int32),
            pltpu.VMEM((MODES, shard), jnp.bfloat16),
            pltpu.VMEM((3, EPOCH_STEPS, COLS), jnp.bfloat16),
            pltpu.SemaphoreType.DMA((CHUNKS + 2,)),
        ],
        compiler_params=LARGE,
        name="spectra",
    )(*(pltpu.with_memory_space_constraint(v, pltpu.HBM) for v in (counts, subspace.T, jnp.asarray(centred_tables()))))

    def from_x(v, k):
        return lax.ppermute(v, "x", [((i + k) % nx, i) for i in range(nx)])

    def to_x(v, k):
        return lax.ppermute(v, "x", [(i, (i + k) % nx) for i in range(nx)])

    def swap(v, axis):
        return lax.ppermute(v, axis, [(0, 1), (1, 0)])

    def both_ways(v, k):
        pairs = [(z, (z + k) % nz) for z in range(nz)] + [(nz + z, nz + (z - k) % nz) for z in range(nz)]
        return lax.ppermute(v, ("c", "z"), pairs)

    first = jnp.concatenate([u, swap(u, "y")], axis=0)
    pair = jnp.concatenate([w, swap(w, "c")], axis=0)
    one = both_ways(pair, 1)
    two = both_ways(pair, 2)
    rows = [first] + [from_x(first, k) for k in range(1, nx)]
    one_c = swap(one, "c")
    two_c = swap(two, "c")
    far = both_ways(jnp.concatenate([one, two[: w.shape[0]]], axis=0), 2)
    far_c = swap(far, "c")
    home, rest = rows[:1], rows[1:]
    near = image(home, [pair], shard)
    near = image(home, [one, one_c, two, two_c], shard, near)
    away = image(rest, [pair, one, one_c], shard)
    away = image(rest, [two, two_c], shard, away)
    away = image(rest, [far], shard, away)
    away = image(rest, [far_c], shard, away)
    back = [to_x(away[k - 1], k) for k in (2, 1, 3)]
    near = image(home, [far, far_c], shard, near)
    mine = add([*near, *back])
    quad = ("y", "c")
    others = [lax.ppermute(mine, quad, [(i, i ^ k) for i in range(4)]) for k in (2, 1, 3)]
    img, grams = gram_of([mine, *others], nx * nz)
    grams = lax.all_to_all(grams, ("x", "z"), 0, 0)
    return modes_of(grams, img, float(np.sqrt(neurons))).T


def solution(mesh):
    fine = Mesh(mesh.devices.reshape(2, 2, 2, 4, 8), ("freq", "y", "c", "x", "z"))
    every = ("freq", "y", "c", "x", "z")

    def body(counts, subspace):
        return local((2, 2, 4, 8), counts, subspace)

    return jax.shard_map(
        body,
        mesh=fine,
        in_specs=(P(every, None, None), P(every, None)),
        out_specs=P(every, None),
        check_vma=False,
    )
```

```python
import functools

import jax
import jax.numpy as jnp
import numpy as np
from jax import lax
from jax.experimental import pallas as pl
from jax.experimental.pallas import tpu as pltpu
from jax.sharding import Mesh
from jax.sharding import PartitionSpec as P

SEGS = 8
TAPERS = 8
EPOCH_STEPS = 128
SPECTRAL_SLOT = 9
MODES = 32
DEGREES = float(SEGS * TAPERS)
COLS = SEGS * 2 * TAPERS
HALF = COLS // 2

SMALL = pltpu.CompilerParams(vmem_limit_bytes=8 << 20)
LARGE = pltpu.CompilerParams(vmem_limit_bytes=24 << 20)


def centred_tables():
    t = np.arange(EPOCH_STEPS, dtype=np.float64)
    k = np.arange(TAPERS, dtype=np.float64) + 1.0
    h = np.sqrt(2.0 / (EPOCH_STEPS + 1.0)) * np.sin(np.pi * (t[:, None] + 1.0) * k[None, :] / (EPOCH_STEPS + 1.0))
    turn = 2.0 * np.pi * SPECTRAL_SLOT * t / EPOCH_STEPS
    re = h * np.cos(turn)[:, None]
    im = -h * np.sin(turn)[:, None]
    re = re - re.mean(axis=0, keepdims=True)
    im = im - im.mean(axis=0, keepdims=True)
    full = np.concatenate([np.tile(re, (1, SEGS)), np.tile(im, (1, SEGS))], axis=1)
    parts = []
    rest = full
    for _ in range(3):
        part = rest.astype(jnp.bfloat16)
        parts.append(part)
        rest = rest - part.astype(np.float64)
    return np.stack(parts, axis=0)


def dot(a, b, ca, cb, precision=None):
    return lax.dot_general(
        a, b, (((ca,), (cb,)), ((), ())), precision=precision, preferred_element_type=jnp.float32
    )


def spectra_kernel(counts_hbm, subspace_hbm, tables_hbm, u_ref, w_ref, counts, subspace, tables, sems):
    rows = counts.shape[1]
    first = pltpu.make_async_copy(tables_hbm, tables, sems.at[SEGS])
    segments = [pltpu.make_async_copy(counts_hbm.at[:, s, :], counts.at[s], sems.at[s]) for s in range(SEGS)]
    last = pltpu.make_async_copy(subspace_hbm, subspace, sems.at[SEGS + 1])
    for copy in (first, *segments, last):
        copy.start()
    segment = lax.broadcasted_iota(jnp.int32, (EPOCH_STEPS, COLS), 1) % HALF // TAPERS
    first.wait()
    table = [
        [jnp.where(segment == s, tables[p].astype(jnp.float32), 0.0).astype(jnp.bfloat16) for p in range(3)]
        for s in range(SEGS)
    ]
    upper = jnp.zeros((rows, 2 * COLS), jnp.float32)
    lower = jnp.zeros((rows, COLS), jnp.float32)
    for s in range(0, SEGS, 2):
        segments[s].wait()
        segments[s + 1].wait()
        x = jnp.concatenate([counts[s + j].astype(jnp.float32).astype(jnp.bfloat16) for j in range(2)], axis=1)
        t = [jnp.concatenate([table[s][p], table[s + 1][p]], axis=0) for p in range(3)]
        upper = upper + dot(x, jnp.concatenate(t[:2], axis=1), 1, 0)
        lower = lower + dot(x, t[2], 1, 0)
    total = upper[:, :COLS] + (upper[:, COLS:] + lower)
    spectra = total.astype(jnp.bfloat16).astype(jnp.float32)
    power = jnp.sum(spectra * spectra, axis=1, keepdims=True) + 1e-05
    scale = jnp.sqrt(np.float32(np.sqrt(DEGREES / (DEGREES - 1.0))) / power)
    u = (spectra * scale).astype(jnp.bfloat16)
    u_ref[...] = u
    w_ref[0:rows, :] = u
    last.wait()
    for j in range(rows // 128):
        w_ref[rows + MODES * j : rows + MODES * (j + 1), :] = subspace[:, 128 * j : 128 * (j + 1)]


def twist(u):
    turned = pltpu.roll(u.astype(jnp.float32), HALF, 1)
    lane = lax.broadcasted_iota(jnp.int32, turned.shape, 1)
    return jnp.where(lane < HALF, turned, -turned).astype(jnp.bfloat16)


def unpack_panels(panels, shard):
    packed = shard + shard // 128 * MODES
    w, st = [], []
    for panel in panels:
        for base in range(0, panel.shape[0], packed):
            w.append(panel[base : base + shard, :])
            st += [panel[base + shard + MODES * j : base + shard + MODES * (j + 1), :] for j in range(shard // 128)]
    return w, st


def coherence(re, im):
    return jnp.maximum(re * re + im * im - np.float32(1.0 / (DEGREES - 1.0)), 0.0).astype(jnp.bfloat16)


def image_kernel(shard, blocks, pieces, has_start, *refs):
    rows = refs[:blocks]
    panels = refs[blocks : blocks + pieces]
    starts = refs[blocks + pieces : 2 * blocks + pieces] if has_start else ()
    outs = refs[-blocks:]
    u = jnp.concatenate([r[...] for r in rows], axis=0)
    t = twist(u)
    if has_start:
        acc = jnp.concatenate([r[...] for r in starts], axis=1)
    else:
        acc = jnp.zeros((MODES, u.shape[0]), jnp.float32)
    w, st = unpack_panels(panels, shard)
    per = len(st) // len(w)
    if u.shape[0] < 1024:
        w = jnp.concatenate(w, axis=0)
        c = coherence(dot(w, u, 1, 1), dot(w, t, 1, 1))
        acc = acc + dot(jnp.concatenate(st, axis=1), c, 1, 0)
    else:
        for k in range(len(w)):
            c = coherence(dot(u, w[k], 1, 1), dot(t, w[k], 1, 1))
            acc = acc + dot(jnp.concatenate(st[k * per : (k + 1) * per], axis=1), c, 1, 1)
    width = rows[0].shape[0]
    for i in range(blocks):
        outs[i][...] = acc[:, i * width : (i + 1) * width]


def image(rows, panels, shard, starts=()):
    n = sum(r.shape[0] for r in rows)
    cols = sum(p.shape[0] for p in panels) * 4 // 5
    return pl.pallas_call(
        functools.partial(image_kernel, shard, len(rows), len(panels), len(starts) > 0),
        out_shape=[jax.ShapeDtypeStruct((MODES, r.shape[0]), jnp.float32) for r in rows],
        compiler_params=LARGE,
        cost_estimate=pl.CostEstimate(
            flops=2 * n * cols * (2 * COLS + 4 * MODES), bytes_accessed=n * 256 + cols * 320, transcendentals=0
        ),
    )(*rows, *panels, *starts)


def add_kernel(*refs):
    total = refs[0][...]
    for r in refs[1:-1]:
        total = total + r[...]
    refs[-1][...] = total


def add(parts):
    return pl.pallas_call(
        add_kernel,
        out_shape=jax.ShapeDtypeStruct(parts[0].shape, jnp.float32),
        compiler_params=SMALL,
        name="add",
    )(*parts)


def pack(g):
    return jnp.concatenate([g[8 * q : 8 * q + 8, :] for q in range(4)], axis=1)


def unpack(g):
    return jnp.concatenate([g[:, 32 * q : 32 * q + 32] for q in range(4)], axis=0)


def gram_kernel(copies, mine, by_y, by_core, by_both, image_ref, gram_ref):
    half = mine.shape[1] // 2
    own = mine[:, :half] + by_y[:, half:]
    image_ref[...] = own
    sums = jnp.concatenate(
        [
            own,
            mine[:, half:] + by_y[:, :half],
            by_core[:, :half] + by_both[:, half:],
            by_core[:, half:] + by_both[:, :half],
        ],
        axis=1,
    )
    g = pack(dot(sums, sums, 1, 1, lax.Precision.HIGHEST))
    for k in range(copies):
        gram_ref[k] = g


def gram_of(parts, copies):
    return pl.pallas_call(
        functools.partial(gram_kernel, copies),
        out_shape=[
            jax.ShapeDtypeStruct((MODES, parts[0].shape[1] // 2), jnp.float32),
            jax.ShapeDtypeStruct((copies, 8, 128), jnp.float32),
        ],
        compiler_params=SMALL,
        name="gram",
    )(*parts)


BLOCK = 4


def modes_kernel(scale, grams, image_ref, out):
    g = unpack(jnp.sum(grams[...], axis=0))
    g = jnp.concatenate([g, jnp.zeros((MODES, 128 - MODES), jnp.float32)], axis=1)
    y = image_ref[...]
    n = y.shape[1]
    for k in range(0, MODES, BLOCK):
        block = [
            [jnp.broadcast_to(g[k + i : k + i + 1, k + j : k + j + 1], (8, 128)) for j in range(i + 1)]
            for i in range(BLOCK)
        ]
        gr = [jnp.broadcast_to(g[k + i : k + i + 1, :], (8, 128)) for i in range(BLOCK)]
        yr = [jnp.broadcast_to(y[k + i : k + i + 1, :], (8, n)) for i in range(BLOCK)]
        gc = [jnp.broadcast_to(g[:, k + i : k + i + 1], (MODES, 128)) for i in range(BLOCK)]
        wide = lambda v: jnp.concatenate([v] * (n // 128), axis=1)
        tall = lambda v: jnp.concatenate([v] * (MODES // 8), axis=0)
        for i in range(BLOCK):
            for j in range(i):
                low = block[i][j]
                for r in range(i, BLOCK):
                    if r == i:
                        block[i][i] = block[i][i] - low * low
                    else:
                        block[r][i] = block[r][i] - block[r][j] * low
                gr[i] = gr[i] - low * gr[j]
                yr[i] = yr[i] - wide(low) * yr[j]
                gc[i] = gc[i] - tall(low) * gc[j]
            pivot = block[i][i]
            inv = lax.rsqrt(pivot)
            inv = inv * (1.5 - 0.5 * pivot * inv * inv)
            for r in range(i + 1, BLOCK):
                block[r][i] = block[r][i] * inv
            gr[i] = gr[i] * inv
            yr[i] = yr[i] * wide(inv)
            gc[i] = gc[i] * tall(inv)
        if k + BLOCK < MODES:
            for i in range(BLOCK):
                g = g - gc[i] * tall(gr[i])
                y = y - wide(gc[i]) * tall(yr[i])
        for i in range(BLOCK):
            out[k + i : k + i + 1, :] = yr[i][0:1, :] * scale


def modes_of(grams, img, scale):
    return pl.pallas_call(
        functools.partial(modes_kernel, scale),
        out_shape=jax.ShapeDtypeStruct((MODES, img.shape[1]), jnp.float32),
        compiler_params=SMALL,
        name="modes",
    )(grams, img)


def local(sizes, counts, subspace):
    ny, nc, nx, nz = sizes
    shard = counts.shape[0]
    neurons = shard * ny * nc * nx * nz
    u, w = pl.pallas_call(
        spectra_kernel,
        out_shape=[
            jax.ShapeDtypeStruct((shard, COLS), jnp.bfloat16),
            jax.ShapeDtypeStruct((shard + shard // 128 * MODES, COLS), jnp.bfloat16),
        ],
        in_specs=[pl.BlockSpec(memory_space=pltpu.HBM)] * 3,
        scratch_shapes=[
            pltpu.VMEM((SEGS, shard, EPOCH_STEPS), jnp.int32),
            pltpu.VMEM((MODES, shard), jnp.bfloat16),
            pltpu.VMEM((3, EPOCH_STEPS, COLS), jnp.bfloat16),
            pltpu.SemaphoreType.DMA((SEGS + 2,)),
        ],
        compiler_params=LARGE,
        name="spectra",
    )(*(pltpu.with_memory_space_constraint(v, pltpu.HBM) for v in (counts, subspace.T, jnp.asarray(centred_tables()))))

    def from_x(v, k):
        return lax.ppermute(v, "x", [((i + k) % nx, i) for i in range(nx)])

    def to_x(v, k):
        return lax.ppermute(v, "x", [(i, (i + k) % nx) for i in range(nx)])

    def swap(v, axis):
        return lax.ppermute(v, axis, [(0, 1), (1, 0)])

    def both_ways(v, k):
        pairs = [(z, (z + k) % nz) for z in range(nz)] + [(nz + z, nz + (z - k) % nz) for z in range(nz)]
        return lax.ppermute(v, ("c", "z"), pairs)

    first = jnp.concatenate([u, swap(u, "y")], axis=0)
    pair = jnp.concatenate([w, swap(w, "c")], axis=0)
    one = both_ways(pair, 1)
    two = both_ways(pair, 2)
    rows = [first] + [from_x(first, k) for k in range(1, nx)]
    ahead = jnp.concatenate([one, two], axis=0)
    far = both_ways(ahead[: 3 * w.shape[0]], 2)
    ahead_c = swap(ahead, "c")
    far_c = swap(far, "c")
    home, rest = rows[:1], rows[1:]
    near = image(home, [pair, one], shard)
    away = image(rest, [pair, ahead], shard)
    away = image(rest, [ahead_c], shard, away)
    away = image(rest, [far], shard, away)
    away = image(rest, [far_c], shard, away)
    back = [to_x(away[k - 1], k) for k in (2, 1, 3)]
    near = image(home, [two, ahead_c, far, far_c], shard, near)
    mine = add([*near, *back])
    quad = ("y", "c")
    others = [lax.ppermute(mine, quad, [(i, i ^ k) for i in range(4)]) for k in (2, 1, 3)]
    img, grams = gram_of([mine, *others], nx * nz)
    grams = lax.all_to_all(grams, ("x", "z"), 0, 0)
    return modes_of(grams, img, float(np.sqrt(neurons))).T


def solution(mesh):
    fine = Mesh(mesh.devices.reshape(2, 2, 2, 4, 8), ("freq", "y", "c", "x", "z"))
    every = ("freq", "y", "c", "x", "z")

    def body(counts, subspace):
        return local((2, 2, 4, 8), counts, subspace)

    return jax.shard_map(
        body,
        mesh=fine,
        in_specs=(P(every, None, None), P(every, None)),
        out_specs=P(every, None),
        check_vma=False,
    )
```

```python
import functools

import jax
import jax.numpy as jnp
import numpy as np
from jax import lax
from jax.experimental import pallas as pl
from jax.experimental.pallas import tpu as pltpu
from jax.sharding import Mesh
from jax.sharding import PartitionSpec as P

SEGS = 8
TAPERS = 8
EPOCH_STEPS = 128
SPECTRAL_SLOT = 9
MODES = 32
DEGREES = float(SEGS * TAPERS)
COLS = SEGS * 2 * TAPERS
HALF = COLS // 2

SMALL = pltpu.CompilerParams(vmem_limit_bytes=8 << 20)
LARGE = pltpu.CompilerParams(vmem_limit_bytes=24 << 20)


def centred_tables():
    t = np.arange(EPOCH_STEPS, dtype=np.float64)
    k = np.arange(TAPERS, dtype=np.float64) + 1.0
    h = np.sqrt(2.0 / (EPOCH_STEPS + 1.0)) * np.sin(np.pi * (t[:, None] + 1.0) * k[None, :] / (EPOCH_STEPS + 1.0))
    turn = 2.0 * np.pi * SPECTRAL_SLOT * t / EPOCH_STEPS
    re = h * np.cos(turn)[:, None]
    im = -h * np.sin(turn)[:, None]
    re = re - re.mean(axis=0, keepdims=True)
    im = im - im.mean(axis=0, keepdims=True)
    full = np.concatenate([np.tile(re, (1, SEGS)), np.tile(im, (1, SEGS))], axis=1)
    parts = []
    rest = full
    for _ in range(3):
        part = rest.astype(jnp.bfloat16)
        parts.append(part)
        rest = rest - part.astype(np.float64)
    return np.stack(parts, axis=0)


def dot(a, b, ca, cb, precision=None):
    return lax.dot_general(
        a, b, (((ca,), (cb,)), ((), ())), precision=precision, preferred_element_type=jnp.float32
    )


def spectra_kernel(counts_hbm, subspace_hbm, tables_hbm, u_ref, w_ref, counts, subspace, tables, sems):
    rows = counts.shape[1]
    first = pltpu.make_async_copy(tables_hbm, tables, sems.at[SEGS])
    segments = [pltpu.make_async_copy(counts_hbm.at[:, s, :], counts.at[s], sems.at[s]) for s in range(SEGS)]
    last = pltpu.make_async_copy(subspace_hbm, subspace, sems.at[SEGS + 1])
    for copy in (first, *segments, last):
        copy.start()
    segment = lax.broadcasted_iota(jnp.int32, (EPOCH_STEPS, COLS), 1) % HALF // TAPERS
    first.wait()
    table = [
        [jnp.where(segment == s, tables[p].astype(jnp.float32), 0.0).astype(jnp.bfloat16) for p in range(3)]
        for s in range(SEGS)
    ]
    upper = jnp.zeros((rows, 2 * COLS), jnp.float32)
    lower = jnp.zeros((rows, COLS), jnp.float32)
    for s in range(0, SEGS, 2):
        segments[s].wait()
        segments[s + 1].wait()
        x = jnp.concatenate([counts[s + j].astype(jnp.float32).astype(jnp.bfloat16) for j in range(2)], axis=1)
        t = [jnp.concatenate([table[s][p], table[s + 1][p]], axis=0) for p in range(3)]
        upper = upper + dot(x, jnp.concatenate(t[:2], axis=1), 1, 0)
        lower = lower + dot(x, t[2], 1, 0)
    total = upper[:, :COLS] + (upper[:, COLS:] + lower)
    spectra = total.astype(jnp.bfloat16).astype(jnp.float32)
    power = jnp.sum(spectra * spectra, axis=1, keepdims=True) + 1e-05
    scale = jnp.sqrt(np.float32(np.sqrt(DEGREES / (DEGREES - 1.0))) / power)
    u = (spectra * scale).astype(jnp.bfloat16)
    u_ref[...] = u
    w_ref[0:rows, :] = u
    last.wait()
    for j in range(rows // 128):
        w_ref[rows + MODES * j : rows + MODES * (j + 1), :] = subspace[:, 128 * j : 128 * (j + 1)]


def twist(u):
    turned = pltpu.roll(u.astype(jnp.float32), HALF, 1)
    lane = lax.broadcasted_iota(jnp.int32, turned.shape, 1)
    return jnp.where(lane < HALF, turned, -turned).astype(jnp.bfloat16)


def unpack_panels(panels, shard):
    packed = shard + shard // 128 * MODES
    w, st = [], []
    for panel in panels:
        for base in range(0, panel.shape[0], packed):
            w.append(panel[base : base + shard, :])
            st += [panel[base + shard + MODES * j : base + shard + MODES * (j + 1), :] for j in range(shard // 128)]
    return w, st


def coherence(re, im):
    return jnp.maximum(re * re + im * im - np.float32(1.0 / (DEGREES - 1.0)), 0.0).astype(jnp.bfloat16)


def image_kernel(shard, blocks, pieces, has_start, *refs):
    rows = refs[:blocks]
    panels = refs[blocks : blocks + pieces]
    starts = refs[blocks + pieces : 2 * blocks + pieces] if has_start else ()
    outs = refs[-blocks:]
    u = jnp.concatenate([r[...] for r in rows], axis=0)
    t = twist(u)
    if has_start:
        acc = jnp.concatenate([r[...] for r in starts], axis=1)
    else:
        acc = jnp.zeros((MODES, u.shape[0]), jnp.float32)
    w, st = unpack_panels(panels, shard)
    per = len(st) // len(w)
    if u.shape[0] < 1024:
        w = jnp.concatenate(w, axis=0)
        c = coherence(dot(w, u, 1, 1), dot(w, t, 1, 1))
        acc = acc + dot(jnp.concatenate(st, axis=1), c, 1, 0)
    else:
        for k in range(len(w)):
            c = coherence(dot(u, w[k], 1, 1), dot(t, w[k], 1, 1))
            acc = acc + dot(jnp.concatenate(st[k * per : (k + 1) * per], axis=1), c, 1, 1)
    width = rows[0].shape[0]
    for i in range(blocks):
        outs[i][...] = acc[:, i * width : (i + 1) * width]


def image(rows, panels, shard, starts=()):
    n = sum(r.shape[0] for r in rows)
    cols = sum(p.shape[0] for p in panels) * 4 // 5
    return pl.pallas_call(
        functools.partial(image_kernel, shard, len(rows), len(panels), len(starts) > 0),
        out_shape=[jax.ShapeDtypeStruct((MODES, r.shape[0]), jnp.float32) for r in rows],
        compiler_params=LARGE,
        cost_estimate=pl.CostEstimate(
            flops=2 * n * cols * (2 * COLS + 4 * MODES), bytes_accessed=n * 256 + cols * 320, transcendentals=0
        ),
    )(*rows, *panels, *starts)


def add_kernel(*refs):
    total = refs[0][...]
    for r in refs[1:-1]:
        total = total + r[...]
    refs[-1][...] = total


def add(parts):
    return pl.pallas_call(
        add_kernel,
        out_shape=jax.ShapeDtypeStruct(parts[0].shape, jnp.float32),
        compiler_params=SMALL,
        name="add",
    )(*parts)


def pack(g):
    return jnp.concatenate([g[8 * q : 8 * q + 8, :] for q in range(4)], axis=1)


def unpack(g):
    return jnp.concatenate([g[:, 32 * q : 32 * q + 32] for q in range(4)], axis=0)


def gram_kernel(copies, mine, by_y, by_core, by_both, image_ref, gram_ref):
    half = mine.shape[1] // 2
    own = mine[:, :half] + by_y[:, half:]
    image_ref[...] = own
    sums = jnp.concatenate(
        [
            own,
            mine[:, half:] + by_y[:, :half],
            by_core[:, :half] + by_both[:, half:],
            by_core[:, half:] + by_both[:, :half],
        ],
        axis=1,
    )
    g = pack(dot(sums, sums, 1, 1, lax.Precision.HIGHEST))
    for k in range(copies):
        gram_ref[k] = g


def gram_of(parts, copies):
    return pl.pallas_call(
        functools.partial(gram_kernel, copies),
        out_shape=[
            jax.ShapeDtypeStruct((MODES, parts[0].shape[1] // 2), jnp.float32),
            jax.ShapeDtypeStruct((copies, 8, 128), jnp.float32),
        ],
        compiler_params=SMALL,
        name="gram",
    )(*parts)


BLOCK = 4


def modes_kernel(scale, grams, image_ref, out):
    g = unpack(jnp.sum(grams[...], axis=0))
    g = jnp.concatenate([g, jnp.zeros((MODES, 128 - MODES), jnp.float32)], axis=1)
    y = image_ref[...]
    n = y.shape[1]
    for k in range(0, MODES, BLOCK):
        block = [
            [jnp.broadcast_to(g[k + i : k + i + 1, k + j : k + j + 1], (8, 128)) for j in range(i + 1)]
            for i in range(BLOCK)
        ]
        gr = [jnp.broadcast_to(g[k + i : k + i + 1, :], (8, 128)) for i in range(BLOCK)]
        yr = [jnp.broadcast_to(y[k + i : k + i + 1, :], (8, n)) for i in range(BLOCK)]
        gc = [jnp.broadcast_to(g[:, k + i : k + i + 1], (MODES, 128)) for i in range(BLOCK)]
        wide = lambda v: jnp.concatenate([v] * (n // 128), axis=1)
        tall = lambda v: jnp.concatenate([v] * (MODES // 8), axis=0)
        for i in range(BLOCK):
            for j in range(i):
                low = block[i][j]
                for r in range(i, BLOCK):
                    if r == i:
                        block[i][i] = block[i][i] - low * low
                    else:
                        block[r][i] = block[r][i] - block[r][j] * low
                gr[i] = gr[i] - low * gr[j]
                yr[i] = yr[i] - wide(low) * yr[j]
                gc[i] = gc[i] - tall(low) * gc[j]
            pivot = block[i][i]
            inv = lax.rsqrt(pivot)
            inv = inv * (1.5 - 0.5 * pivot * inv * inv)
            for r in range(i + 1, BLOCK):
                block[r][i] = block[r][i] * inv
            gr[i] = gr[i] * inv
            yr[i] = yr[i] * wide(inv)
            gc[i] = gc[i] * tall(inv)
        if k + BLOCK < MODES:
            for i in range(BLOCK):
                g = g - gc[i] * tall(gr[i])
                y = y - wide(gc[i]) * tall(yr[i])
        for i in range(BLOCK):
            out[k + i : k + i + 1, :] = yr[i][0:1, :] * scale


def modes_of(grams, img, scale):
    return pl.pallas_call(
        functools.partial(modes_kernel, scale),
        out_shape=jax.ShapeDtypeStruct((MODES, img.shape[1]), jnp.float32),
        compiler_params=SMALL,
        name="modes",
    )(grams, img)


def local(sizes, counts, subspace):
    ny, nc, nx, nz = sizes
    shard = counts.shape[0]
    neurons = shard * ny * nc * nx * nz
    u, w = pl.pallas_call(
        spectra_kernel,
        out_shape=[
            jax.ShapeDtypeStruct((shard, COLS), jnp.bfloat16),
            jax.ShapeDtypeStruct((shard + shard // 128 * MODES, COLS), jnp.bfloat16),
        ],
        in_specs=[pl.BlockSpec(memory_space=pltpu.HBM)] * 3,
        scratch_shapes=[
            pltpu.VMEM((SEGS, shard, EPOCH_STEPS), jnp.int32),
            pltpu.VMEM((MODES, shard), jnp.bfloat16),
            pltpu.VMEM((3, EPOCH_STEPS, COLS), jnp.bfloat16),
            pltpu.SemaphoreType.DMA((SEGS + 2,)),
        ],
        compiler_params=LARGE,
        name="spectra",
    )(*(pltpu.with_memory_space_constraint(v, pltpu.HBM) for v in (counts, subspace.T, jnp.asarray(centred_tables()))))

    def from_x(v, k):
        return lax.ppermute(v, "x", [((i + k) % nx, i) for i in range(nx)])

    def to_x(v, k):
        return lax.ppermute(v, "x", [(i, (i + k) % nx) for i in range(nx)])

    def swap(v, axis):
        return lax.ppermute(v, axis, [(0, 1), (1, 0)])

    def both_ways(v, k):
        pairs = [(z, (z + k) % nz) for z in range(nz)] + [(nz + z, nz + (z - k) % nz) for z in range(nz)]
        return lax.ppermute(v, ("c", "z"), pairs)

    first = jnp.concatenate([u, swap(u, "y")], axis=0)
    pair = jnp.concatenate([w, swap(w, "c")], axis=0)
    one = both_ways(pair, 1)
    two = both_ways(pair, 2)
    rows = [first] + [from_x(first, k) for k in range(1, nx)]
    ahead = jnp.concatenate([one, two], axis=0)
    far = both_ways(ahead[: 3 * w.shape[0]], 2)
    ahead_c = swap(ahead, "c")
    far_c = swap(far, "c")
    home, rest = rows[:1], rows[1:]
    near = image(home, [pair, one], shard)
    away = image(rest, [pair, ahead], shard)
    away = image(rest, [ahead_c], shard, away)
    away = image(rest, [far], shard, away)
    (two_away,) = image(rest[1:2], [far_c], shard, away[1:2])
    one_away, three_away = image(rest[0::2], [far_c], shard, away[0::2])
    back = [to_x(two_away, 2), to_x(one_away, 1), to_x(three_away, 3)]
    near = image(home, [two, ahead_c, far, far_c], shard, near)
    mine = add([*near, *back])
    quad = ("y", "c")
    others = [lax.ppermute(mine, quad, [(i, i ^ k) for i in range(4)]) for k in (2, 1, 3)]
    img, grams = gram_of([mine, *others], nx * nz)
    grams = lax.all_to_all(grams, ("x", "z"), 0, 0)
    return modes_of(grams, img, float(np.sqrt(neurons))).T


def solution(mesh):
    fine = Mesh(mesh.devices.reshape(2, 2, 2, 4, 8), ("freq", "y", "c", "x", "z"))
    every = ("freq", "y", "c", "x", "z")

    def body(counts, subspace):
        return local((2, 2, 4, 8), counts, subspace)

    return jax.shard_map(
        body,
        mesh=fine,
        in_specs=(P(every, None, None), P(every, None)),
        out_specs=P(every, None),
        check_vma=False,
    )
```

```python
import functools

import jax
import jax.numpy as jnp
import numpy as np
from jax import lax
from jax.experimental import pallas as pl
from jax.experimental.pallas import tpu as pltpu
from jax.sharding import Mesh
from jax.sharding import PartitionSpec as P

SEGS = 8
TAPERS = 8
EPOCH_STEPS = 128
SPECTRAL_SLOT = 9
MODES = 32
DEGREES = float(SEGS * TAPERS)
COLS = SEGS * 2 * TAPERS
HALF = COLS // 2

SMALL = pltpu.CompilerParams(vmem_limit_bytes=8 << 20)
LARGE = pltpu.CompilerParams(vmem_limit_bytes=24 << 20)


def centred_tables():
    t = np.arange(EPOCH_STEPS, dtype=np.float64)
    k = np.arange(TAPERS, dtype=np.float64) + 1.0
    h = np.sqrt(2.0 / (EPOCH_STEPS + 1.0)) * np.sin(np.pi * (t[:, None] + 1.0) * k[None, :] / (EPOCH_STEPS + 1.0))
    turn = 2.0 * np.pi * SPECTRAL_SLOT * t / EPOCH_STEPS
    re = h * np.cos(turn)[:, None]
    im = -h * np.sin(turn)[:, None]
    re = re - re.mean(axis=0, keepdims=True)
    im = im - im.mean(axis=0, keepdims=True)
    full = np.concatenate([np.tile(re, (1, SEGS)), np.tile(im, (1, SEGS))], axis=1)
    parts = []
    rest = full
    for _ in range(3):
        part = rest.astype(jnp.bfloat16)
        parts.append(part)
        rest = rest - part.astype(np.float64)
    return np.stack(parts, axis=0)


def dot(a, b, ca, cb, precision=None):
    return lax.dot_general(
        a, b, (((ca,), (cb,)), ((), ())), precision=precision, preferred_element_type=jnp.float32
    )


def spectra_kernel(counts_hbm, subspace_hbm, tables_hbm, u_ref, w_ref, counts, subspace, tables, sems):
    rows = counts.shape[1]
    first = pltpu.make_async_copy(tables_hbm, tables, sems.at[SEGS])
    segments = [pltpu.make_async_copy(counts_hbm.at[:, s, :], counts.at[s], sems.at[s]) for s in range(SEGS)]
    last = pltpu.make_async_copy(subspace_hbm, subspace, sems.at[SEGS + 1])
    for copy in (first, *segments, last):
        copy.start()
    segment = lax.broadcasted_iota(jnp.int32, (EPOCH_STEPS, COLS), 1) % HALF // TAPERS
    first.wait()
    table = [
        [jnp.where(segment == s, tables[p].astype(jnp.float32), 0.0).astype(jnp.bfloat16) for p in range(3)]
        for s in range(SEGS)
    ]
    upper = jnp.zeros((rows, 2 * COLS), jnp.float32)
    lower = jnp.zeros((rows, COLS), jnp.float32)
    for s in range(0, SEGS, 2):
        segments[s].wait()
        segments[s + 1].wait()
        x = jnp.concatenate([counts[s + j].astype(jnp.float32).astype(jnp.bfloat16) for j in range(2)], axis=1)
        t = [jnp.concatenate([table[s][p], table[s + 1][p]], axis=0) for p in range(3)]
        upper = upper + dot(x, jnp.concatenate(t[:2], axis=1), 1, 0)
        lower = lower + dot(x, t[2], 1, 0)
    total = upper[:, :COLS] + (upper[:, COLS:] + lower)
    spectra = total.astype(jnp.bfloat16).astype(jnp.float32)
    power = jnp.sum(spectra * spectra, axis=1, keepdims=True) + 1e-05
    scale = jnp.sqrt(np.float32(np.sqrt(DEGREES / (DEGREES - 1.0))) / power)
    u = (spectra * scale).astype(jnp.bfloat16)
    u_ref[...] = u
    w_ref[0:rows, :] = u
    last.wait()
    for j in range(rows // 128):
        w_ref[rows + MODES * j : rows + MODES * (j + 1), :] = subspace[:, 128 * j : 128 * (j + 1)]


def twist(u):
    turned = pltpu.roll(u.astype(jnp.float32), HALF, 1)
    lane = lax.broadcasted_iota(jnp.int32, turned.shape, 1)
    return jnp.where(lane < HALF, turned, -turned).astype(jnp.bfloat16)


def unpack_panels(panels, shard):
    packed = shard + shard // 128 * MODES
    w, st = [], []
    for panel in panels:
        for base in range(0, panel.shape[0], packed):
            w.append(panel[base : base + shard, :])
            st += [panel[base + shard + MODES * j : base + shard + MODES * (j + 1), :] for j in range(shard // 128)]
    return w, st


def coherence(re, im):
    return jnp.maximum(re * re + im * im - np.float32(1.0 / (DEGREES - 1.0)), 0.0).astype(jnp.bfloat16)


def image_kernel(shard, blocks, pieces, has_start, *refs):
    rows = refs[:blocks]
    panels = refs[blocks : blocks + pieces]
    starts = refs[blocks + pieces : 2 * blocks + pieces] if has_start else ()
    outs = refs[-blocks:]
    u = jnp.concatenate([r[...] for r in rows], axis=0)
    t = twist(u)
    if has_start:
        acc = jnp.concatenate([r[...] for r in starts], axis=1)
    else:
        acc = jnp.zeros((MODES, u.shape[0]), jnp.float32)
    w, st = unpack_panels(panels, shard)
    per = len(st) // len(w)
    if u.shape[0] < 1024:
        w = jnp.concatenate(w, axis=0)
        c = coherence(dot(w, u, 1, 1), dot(w, t, 1, 1))
        acc = acc + dot(jnp.concatenate(st, axis=1), c, 1, 0)
    else:
        for k in range(len(w)):
            c = coherence(dot(u, w[k], 1, 1), dot(t, w[k], 1, 1))
            acc = acc + dot(jnp.concatenate(st[k * per : (k + 1) * per], axis=1), c, 1, 1)
    width = rows[0].shape[0]
    for i in range(blocks):
        outs[i][...] = acc[:, i * width : (i + 1) * width]


def image(rows, panels, shard, starts=()):
    n = sum(r.shape[0] for r in rows)
    cols = sum(p.shape[0] for p in panels) * 4 // 5
    return pl.pallas_call(
        functools.partial(image_kernel, shard, len(rows), len(panels), len(starts) > 0),
        out_shape=[jax.ShapeDtypeStruct((MODES, r.shape[0]), jnp.float32) for r in rows],
        compiler_params=LARGE,
        cost_estimate=pl.CostEstimate(
            flops=2 * n * cols * (2 * COLS + 4 * MODES), bytes_accessed=n * 256 + cols * 320, transcendentals=0
        ),
    )(*rows, *panels, *starts)


def add_kernel(*refs):
    total = refs[0][...]
    for r in refs[1:-1]:
        total = total + r[...]
    refs[-1][...] = total


def add(parts):
    return pl.pallas_call(
        add_kernel,
        out_shape=jax.ShapeDtypeStruct(parts[0].shape, jnp.float32),
        compiler_params=SMALL,
        name="add",
    )(*parts)


def pack(g):
    return jnp.concatenate([g[8 * q : 8 * q + 8, :] for q in range(4)], axis=1)


def unpack(g):
    return jnp.concatenate([g[:, 32 * q : 32 * q + 32] for q in range(4)], axis=0)


def gram_kernel(copies, mine, by_y, by_core, by_both, image_ref, gram_ref):
    half = mine.shape[1] // 2
    own = mine[:, :half] + by_y[:, half:]
    image_ref[...] = own
    sums = jnp.concatenate(
        [
            own,
            mine[:, half:] + by_y[:, :half],
            by_core[:, :half] + by_both[:, half:],
            by_core[:, half:] + by_both[:, :half],
        ],
        axis=1,
    )
    g = pack(dot(sums, sums, 1, 1, lax.Precision.HIGHEST))
    for k in range(copies):
        gram_ref[k] = g


def gram_of(parts, copies):
    return pl.pallas_call(
        functools.partial(gram_kernel, copies),
        out_shape=[
            jax.ShapeDtypeStruct((MODES, parts[0].shape[1] // 2), jnp.float32),
            jax.ShapeDtypeStruct((copies, 8, 128), jnp.float32),
        ],
        compiler_params=SMALL,
        name="gram",
    )(*parts)


BLOCK = 4


def modes_kernel(scale, grams, image_ref, out):
    g = unpack(jnp.sum(grams[...], axis=0))
    g = jnp.concatenate([g, jnp.zeros((MODES, 128 - MODES), jnp.float32)], axis=1)
    y = image_ref[...]
    n = y.shape[1]
    for k in range(0, MODES, BLOCK):
        block = [
            [jnp.broadcast_to(g[k + i : k + i + 1, k + j : k + j + 1], (8, 128)) for j in range(i + 1)]
            for i in range(BLOCK)
        ]
        gr = [jnp.broadcast_to(g[k + i : k + i + 1, :], (8, 128)) for i in range(BLOCK)]
        yr = [jnp.broadcast_to(y[k + i : k + i + 1, :], (8, n)) for i in range(BLOCK)]
        gc = [jnp.broadcast_to(g[:, k + i : k + i + 1], (MODES, 128)) for i in range(BLOCK)]
        wide = lambda v: jnp.concatenate([v] * (n // 128), axis=1)
        tall = lambda v: jnp.concatenate([v] * (MODES // 8), axis=0)
        for i in range(BLOCK):
            for j in range(i):
                low = block[i][j]
                for r in range(i, BLOCK):
                    if r == i:
                        block[i][i] = block[i][i] - low * low
                    else:
                        block[r][i] = block[r][i] - block[r][j] * low
                gr[i] = gr[i] - low * gr[j]
                yr[i] = yr[i] - wide(low) * yr[j]
                gc[i] = gc[i] - tall(low) * gc[j]
            pivot = block[i][i]
            inv = lax.rsqrt(pivot)
            inv = inv * (1.5 - 0.5 * pivot * inv * inv)
            for r in range(i + 1, BLOCK):
                block[r][i] = block[r][i] * inv
            gr[i] = gr[i] * inv
            yr[i] = yr[i] * wide(inv)
            gc[i] = gc[i] * tall(inv)
        if k + BLOCK < MODES:
            for i in range(BLOCK):
                g = g - gc[i] * tall(gr[i])
                y = y - wide(gc[i]) * tall(yr[i])
        for i in range(BLOCK):
            out[k + i : k + i + 1, :] = yr[i][0:1, :] * scale


def modes_of(grams, img, scale):
    return pl.pallas_call(
        functools.partial(modes_kernel, scale),
        out_shape=jax.ShapeDtypeStruct((MODES, img.shape[1]), jnp.float32),
        compiler_params=SMALL,
        name="modes",
    )(grams, img)


def local(sizes, counts, subspace):
    ny, nc, nx, nz = sizes
    shard = counts.shape[0]
    neurons = shard * ny * nc * nx * nz
    u, w = pl.pallas_call(
        spectra_kernel,
        out_shape=[
            jax.ShapeDtypeStruct((shard, COLS), jnp.bfloat16),
            jax.ShapeDtypeStruct((shard + shard // 128 * MODES, COLS), jnp.bfloat16),
        ],
        in_specs=[pl.BlockSpec(memory_space=pltpu.HBM)] * 3,
        scratch_shapes=[
            pltpu.VMEM((SEGS, shard, EPOCH_STEPS), jnp.int32),
            pltpu.VMEM((MODES, shard), jnp.bfloat16),
            pltpu.VMEM((3, EPOCH_STEPS, COLS), jnp.bfloat16),
            pltpu.SemaphoreType.DMA((SEGS + 2,)),
        ],
        compiler_params=LARGE,
        name="spectra",
    )(*(pltpu.with_memory_space_constraint(v, pltpu.HBM) for v in (counts, subspace.T, jnp.asarray(centred_tables()))))

    def from_x(v, k):
        return lax.ppermute(v, "x", [((i + k) % nx, i) for i in range(nx)])

    def to_x(v, k):
        return lax.ppermute(v, "x", [(i, (i + k) % nx) for i in range(nx)])

    def swap(v, axis):
        return lax.ppermute(v, axis, [(0, 1), (1, 0)])

    def both_ways(v, k):
        pairs = [(z, (z + k) % nz) for z in range(nz)] + [(nz + z, nz + (z - k) % nz) for z in range(nz)]
        return lax.ppermute(v, ("c", "z"), pairs)

    first = jnp.concatenate([u, swap(u, "y")], axis=0)
    pair = jnp.concatenate([w, swap(w, "c")], axis=0)
    one = both_ways(pair, 1)
    two = both_ways(pair, 2)
    rows = [first] + [from_x(first, k) for k in range(1, nx)]
    three = both_ways(one, 2)
    four = both_ways(two[: w.shape[0]], 2)
    ahead_c = swap(jnp.concatenate([one, two], axis=0), "c")
    three_c = swap(three, "c")
    four_c = swap(four, "c")
    home, rest = rows[:1], rows[1:]
    near = image(home, [pair, one], shard)
    away = image(rest, [pair, one, two], shard)
    away = image(rest, [ahead_c], shard, away)
    away = image(rest, [three, three_c], shard, away)
    away = image(rest, [four, four_c], shard, away)
    back = [to_x(away[k - 1], k) for k in (2, 1, 3)]
    near = image(home, [two, ahead_c, three, three_c, four, four_c], shard, near)
    mine = add([*near, *back])
    quad = ("y", "c")
    others = [lax.ppermute(mine, quad, [(i, i ^ k) for i in range(4)]) for k in (2, 1, 3)]
    img, grams = gram_of([mine, *others], nx * nz)
    grams = lax.all_to_all(grams, ("x", "z"), 0, 0)
    return modes_of(grams, img, float(np.sqrt(neurons))).T


def solution(mesh):
    fine = Mesh(mesh.devices.reshape(2, 2, 2, 4, 8), ("freq", "y", "c", "x", "z"))
    every = ("freq", "y", "c", "x", "z")

    def body(counts, subspace):
        return local((2, 2, 4, 8), counts, subspace)

    return jax.shard_map(
        body,
        mesh=fine,
        in_specs=(P(every, None, None), P(every, None)),
        out_specs=P(every, None),
        check_vma=False,
    )
```
